32 devices in a mesh: dom: 8 (over z, x), sub: 4 (over y, core).
Axes of the slice: x: 2, y: 2, z: 4, core: 2. Of those that a mesh axis runs over, the one named last changes fastest.
Arguments:
- positions: float32 [3, 1048576], P(None, ('dom', 'sub')), may hold values from -0.11 to 1.11
- velocities: float32 [3, 1048576], P(None, ('dom', 'sub')), may hold values from -3 to 3
- masses: float32 [1048576], P(('dom', 'sub')), may hold values from 0.003 to 0.012
- accel_prev: float32 [3, 1048576], P(None, ('dom', 'sub')), may hold values from -180 to 180
- active: int32 [1048576], P(('dom', 'sub')), may hold values from 0 to 1, as said below
- bucket_top: int32 [4096], P(('dom', 'sub')), may hold values from 0 to 4095
- near_list: int32 [4096, 4], P(('dom', 'sub')), may hold values from 0 to 511, as said below
- cell_list: int32 [4096, 64], P(('dom', 'sub')), may hold values from 0 to 1023
- top_list: int32 [4096, 32], P(('dom', 'sub')), may hold values from 0 to 4095
- essential: int32 [8, 4, 8, 32], P('dom', 'sub'), may hold values from 0 to 511
- work: int32 [1280], P(('dom', 'sub')), may hold values from 0 to 511, as said below
Outputs:
- vel_out: float32 [3, 1048576], P(None, ('dom', 'sub'))
- pos_out: float32 [3, 1048576], P(None, ('dom', 'sub'))
The draws below stay inside these ranges and needn't reach their ends.
Inputs may be any that keep to these rules, and one draw needn't show every extreme that they name: near_list[n, 0] is the group-local number of bucket n itself; every entry of row n names a bucket of n's group whose top cell differs from n's by at most one in each of the three top-cell coordinates. A bucket holds an active particle exactly when its group-local number appears in its group's block of work. `work`: entries g * 4 * 40 to (g + 1) * 4 * 40 - 1 are the block of domain group g and name distinct group-local buckets; in every group one device holds 128 of the named buckets.
All inputs are finite; a program needn't handle non-finite values.
Results may differ from the reference program's by a relative error of at most 0.0003.
Values sent between devices are 32-bit elements; how exact they have to be, the bound alone decides.
No kernel may reach another device: no remote copies, remote signals or barrier semaphores. Data moves between devices by JAX's collectives and lax.ppermute only.
A program may use at most 64 MiB of HBM per device.

```python
import math
import jax
import jax.numpy as jnp
from jax import lax

BUCKET = 256
B_DEV = 128
W_DEV = 40
RS = 32
NB = 4
NC = 64
NT = 32
TOP_SIDE = 16
STEPS = 2
TOP = 4096
G_BUCK = 512
NBUCK = 4096
NPART = 1048576
ESS = 1024
N_DOM = 8
N_SUB = 4


def activity_plan(base_key):
    group_keys = jax.random.split(base_key, N_DOM)

    def one_group(group_key):
        key_busy, key_select, key_shuffle = jax.random.split(group_key, 3)
        busiest = jax.random.randint(key_busy, (), 0, N_SUB)
        remaining = N_SUB * W_DEV - B_DEV
        selected = jax.random.permutation(key_select, (N_SUB - 1) * B_DEV)[:remaining].astype(jnp.int32)
        others = selected + B_DEV * (selected >= B_DEV * busiest).astype(jnp.int32)
        starred = busiest * B_DEV + jnp.arange(B_DEV, dtype=jnp.int32)
        chosen = jnp.concatenate([starred, others]).astype(jnp.int32)
        shuffled = jax.random.permutation(key_shuffle, chosen)
        bucket_marks = jnp.zeros((G_BUCK,), jnp.int32).at[chosen].set(1)
        return (shuffled.astype(jnp.int32), bucket_marks)
    return jax.vmap(one_group)(group_keys)


def draw_work(key, part):
    shuffled, bucket_marks = activity_plan(jax.random.fold_in(key, 11))
    return shuffled.reshape(-1).astype(jnp.int32)


def draw_active(key, part):
    shuffled, bucket_marks = activity_plan(jax.random.fold_in(key, 11))
    coin_flips = jax.random.randint(jax.random.fold_in(key, 12), (NBUCK, BUCKET), 0, 2)
    chosen_lane = jax.random.randint(jax.random.fold_in(key, 13), (NBUCK, 1), 0, BUCKET)
    lane_ids = jnp.arange(BUCKET, dtype=jnp.int32)[None, :]
    flags = jnp.maximum(coin_flips, (lane_ids == chosen_lane).astype(jnp.int32))
    flags = flags * bucket_marks.reshape(NBUCK, 1)
    return flags.reshape(-1).astype(jnp.int32)


def bucket_plan(base_key):
    cell_side = TOP_SIDE
    cluster_span = 4
    cluster_count = G_BUCK // cluster_span
    group_keys = jax.random.split(jax.random.fold_in(base_key, 21), N_DOM)
    starts = jax.random.randint(jax.random.fold_in(base_key, 24), (N_DOM, 3), 0, cell_side).astype(jnp.int32)
    starts = starts.at[0].set(0).at[N_DOM - 1].set(cell_side - 1)

    def one_group(group_key, start):
        key_order, key_moves, key_reach, key_sides = jax.random.split(group_key, 4)
        order = jax.random.permutation(key_order, G_BUCK).astype(jnp.int32)
        moves = jax.random.randint(key_moves, (3, cluster_count), -1, 2).astype(jnp.int32)
        moves = moves.at[:, 0].set(0)
        walk = jnp.clip(start[:, None] + jnp.cumsum(moves, axis=1), 0, cell_side - 1)
        cluster_top = (walk[0] * cell_side * cell_side + walk[1] * cell_side + walk[2]).astype(jnp.int32)
        slot_ids = jnp.arange(G_BUCK, dtype=jnp.int32)
        slot_top = cluster_top[slot_ids // cluster_span]
        reach = jax.random.randint(key_reach, (G_BUCK, NB - 1), 1, cluster_span + 1).astype(jnp.int32)
        sides = 2 * jax.random.randint(key_sides, (G_BUCK, NB - 1), 0, 2).astype(jnp.int32) - 1
        near_slots = jnp.clip(slot_ids[:, None] + reach * sides, 0, G_BUCK - 1)
        rows = jnp.concatenate([order[:, None], order[near_slots]], axis=1).astype(jnp.int32)
        tops = jnp.zeros((G_BUCK,), jnp.int32).at[order].set(slot_top)
        nearby = jnp.zeros((G_BUCK, NB), jnp.int32).at[order].set(rows)
        return (tops, nearby)
    tops, nearby = jax.vmap(one_group)(group_keys, starts)
    return (tops.reshape(NBUCK).astype(jnp.int32), nearby.reshape(NBUCK, NB).astype(jnp.int32))


def draw_bucket_top(key, part):
    tops, nearby = bucket_plan(key)
    return tops


def draw_near_list(key, part):
    tops, nearby = bucket_plan(key)
    return nearby


def draw_positions(key, part):
    top_ids, nearby = bucket_plan(key)
    cell_side = TOP_SIDE
    first_index = top_ids // (cell_side * cell_side)
    second_index = top_ids // cell_side % cell_side
    third_index = top_ids % cell_side
    centres = (jnp.stack([first_index, second_index, third_index]).astype(jnp.float32) + 0.5) / cell_side
    jitter = jax.random.uniform(jax.random.fold_in(key, 22), (3, NBUCK, 1), jnp.float32, -0.5, 0.5) / cell_side
    spread = 0.03 * jnp.clip(jax.random.normal(jax.random.fold_in(key, 23), (3, NBUCK, BUCKET), jnp.float32), -3.5, 3.5)
    places = centres[:, :, None] + jitter + spread
    return places.reshape(3, NPART).astype(jnp.float32)


def plant(values, own_key, low, high):
    spot = [jax.random.randint(jax.random.fold_in(own_key, axis), (), 0, length) for axis, length in enumerate(values.shape)]
    longest = values.shape.index(max(values.shape))
    beside = spot[:longest] + [(spot[longest] + 1) % values.shape[longest]] + spot[longest + 1:]
    return values.at[tuple(spot)].set(low).at[tuple(beside)].set(high)


def levels(key, extent, pieces, least, high):
    factor_of = 1.0
    for position, blocks in pieces:
        steps = jax.random.uniform(jax.random.fold_in(jax.random.fold_in(key, 6), position), (blocks,), jnp.float32, least / len(pieces), high / len(pieces))
        factor_of = factor_of * jnp.repeat(jnp.exp(steps), extent[position] // blocks).reshape((-1,) + (1,) * (len(extent) - 1 - position))
    return factor_of


def noise(key, shape, width, bound, cuts=(), kind=jnp.bfloat16):
    values = jax.random.normal(key, shape, jnp.float32) * width
    if len(cuts) > 0:
        values = levels(key, shape, cuts, -0.22, 0.18) * values
    return jnp.clip(values, min=-bound, max=bound).astype(kind)


def setup_inputs(seed: int = 0) -> dict:
    splits = jax.random.split(jax.random.key(seed), 12)
    positions = draw_positions(jax.random.fold_in(splits[11], 71), 0)
    velocities = noise(splits[1], (3, NPART), 0.5, 3.0, ((1, 32),), jnp.float32)
    masses = jnp.clip(jnp.exp(math.log(0.012) - 1.3862944 * jax.random.uniform(splits[2], (NPART,), jnp.float32) ** levels(splits[2], (NPART,), ((0, 32),), -0.2, 0.2)), 0.003, 0.012)
    accel_prev = noise(splits[3], (3, NPART), 30.0, 180.0, ((1, 32),), jnp.float32)
    active = draw_active(jax.random.fold_in(splits[11], 71), 0)
    bucket_top = draw_bucket_top(jax.random.fold_in(splits[11], 71), 0)
    near_list = draw_near_list(jax.random.fold_in(splits[11], 71), 0)
    cell_list = plant(jax.random.randint(splits[7], (NBUCK, NC), 0, ESS), jax.random.fold_in(splits[7], 1), 0, ESS - 1).astype(jnp.int32)
    top_list = plant(jax.random.randint(splits[8], (NBUCK, NT), 0, TOP), jax.random.fold_in(splits[8], 1), 0, TOP - 1).astype(jnp.int32)
    essential = plant(jax.random.randint(splits[9], (N_DOM, N_SUB, N_DOM, RS), 0, G_BUCK), jax.random.fold_in(splits[9], 1), 0, G_BUCK - 1).astype(jnp.int32)
    work = draw_work(jax.random.fold_in(splits[11], 71), 0)
    return dict(positions=positions, velocities=velocities, masses=masses, accel_prev=accel_prev, active=active, bucket_top=bucket_top, near_list=near_list, cell_list=cell_list, top_list=top_list, essential=essential, work=work)


time_step = 0.01
soften = 0.0025
mass_floor = 0.5

def top_centres(top_ids):
    cell_side = TOP_SIDE
    first_index = top_ids // (cell_side * cell_side)
    second_index = top_ids // cell_side % cell_side
    third_index = top_ids % cell_side
    stacked = jnp.stack([first_index, second_index, third_index]).astype(jnp.float32)
    return (stacked + 0.5) / cell_side

def bucket_moments(places, weights):
    mass_total = lax.optimization_barrier(jnp.sum(weights, axis=1))
    centre = lax.optimization_barrier(jnp.sum(places * weights[None], axis=2)) / mass_total[None]
    offsets = places - centre[:, :, None]
    radius_sq = lax.optimization_barrier(jnp.sum(offsets * offsets, axis=0))

    def diagonal(first_axis):
        return lax.optimization_barrier(jnp.sum(weights * (3.0 * offsets[first_axis] * offsets[first_axis] - radius_sq), axis=1))

    def crossed(first_axis, second_axis):
        return 3.0 * lax.optimization_barrier(jnp.sum(weights * offsets[first_axis] * offsets[second_axis], axis=1))
    quadrupole = jnp.stack([diagonal(0), diagonal(1), diagonal(2), crossed(0, 1), crossed(0, 2), crossed(1, 2)])
    return jnp.concatenate([mass_total[None], centre, quadrupole], axis=0)

def top_raw(places, weights, centres):
    offsets = places - centres[:, :, None]
    weighted = weights[None] * offsets
    row_list = [weights, weighted[0], weighted[1], weighted[2], weighted[0] * offsets[0], weighted[1] * offsets[1], weighted[2] * offsets[2], weighted[0] * offsets[1], weighted[0] * offsets[2], weighted[1] * offsets[2]]
    return jnp.stack([lax.optimization_barrier(jnp.sum(row_values, axis=1)) for row_values in row_list])

def top_moments(raw_sums, centres):
    mass_total = raw_sums[0]
    safe_mass = jnp.maximum(mass_total, mass_floor)
    first_sums = raw_sums[1:4]
    centre = centres + first_sums / safe_mass[None]
    cov_xx = raw_sums[4] - first_sums[0] * first_sums[0] / safe_mass
    cov_yy = raw_sums[5] - first_sums[1] * first_sums[1] / safe_mass
    cov_zz = raw_sums[6] - first_sums[2] * first_sums[2] / safe_mass
    cov_xy = raw_sums[7] - first_sums[0] * first_sums[1] / safe_mass
    cov_xz = raw_sums[8] - first_sums[0] * first_sums[2] / safe_mass
    cov_yz = raw_sums[9] - first_sums[1] * first_sums[2] / safe_mass
    trace_sum = cov_xx + cov_yy + cov_zz
    quadrupole = jnp.stack([3.0 * cov_xx - trace_sum, 3.0 * cov_yy - trace_sum, 3.0 * cov_zz - trace_sum, 3.0 * cov_xy, 3.0 * cov_xz, 3.0 * cov_yz])
    return jnp.concatenate([mass_total[None], centre, quadrupole], axis=0)

def pair_accel(targets, sources, source_mass):
    offsets = sources[:, :, None] - targets[:, None, :]
    distance = lax.optimization_barrier(jnp.sum(offsets * offsets, axis=0)) + soften
    inverse = lax.rsqrt(distance)
    strength = source_mass[:, None] * inverse * inverse * inverse
    return lax.optimization_barrier(jnp.sum(offsets * strength[None], axis=1))

def cell_accel(targets, moments):
    offsets = targets[:, None, :] - moments[1:4, :, None]
    distance = lax.optimization_barrier(jnp.sum(offsets * offsets, axis=0)) + soften
    inverse = lax.rsqrt(distance)
    inverse_sq = inverse * inverse
    inverse_three = inverse * inverse_sq
    inverse_five = inverse_three * inverse_sq
    inverse_seven = inverse_five * inverse_sq
    quadrupole = moments[4:10, :, None]
    along_x = quadrupole[0] * offsets[0] + quadrupole[3] * offsets[1] + quadrupole[4] * offsets[2]
    along_y = quadrupole[3] * offsets[0] + quadrupole[1] * offsets[1] + quadrupole[5] * offsets[2]
    along_z = quadrupole[4] * offsets[0] + quadrupole[5] * offsets[1] + quadrupole[2] * offsets[2]
    contracted = offsets[0] * along_x + offsets[1] * along_y + offsets[2] * along_z
    radial = -moments[0][:, None] * inverse_three - 2.5 * contracted * inverse_seven
    along_all = jnp.stack([along_x, along_y, along_z])
    return lax.optimization_barrier(jnp.sum(offsets * radial[None] + along_all * inverse_five[None], axis=1))

def force_one(target, near_ids, cell_ids, top_ids, group_places, group_mass, essential_cells, top_cells):
    sources = group_places[:, near_ids].reshape(3, -1)
    source_mass = group_mass[near_ids].reshape(-1)
    moments = jnp.concatenate([jnp.take(essential_cells, cell_ids, axis=1), jnp.take(top_cells, top_ids, axis=1)], axis=1)
    return pair_accel(target, sources, source_mass) + cell_accel(target, moments)

def in_blocks(step_function, inputs, item_count):
    block_width = 4 if item_count % 4 == 0 else 2 if item_count % 2 == 0 else 1

    def reshape_leaf(values):
        return values.reshape((item_count // block_width, block_width) + values.shape[1:])
    result = lax.map(jax.vmap(step_function), jax.tree.map(reshape_leaf, inputs))
    return result.reshape((item_count,) + result.shape[2:])

def reference(positions, velocities, masses, accel_prev, active, bucket_top, near_list, cell_list, top_list, essential, work):
    activity = active.astype(jnp.float32)
    group_offsets = jnp.arange(N_DOM, dtype=jnp.int32) * G_BUCK
    essential_ids = (essential + group_offsets[None, None, :, None]).reshape(N_DOM, ESS).astype(jnp.int32)
    work_groups = jnp.repeat(jnp.arange(N_DOM, dtype=jnp.int32), N_SUB * W_DEV)
    work_global = (work + work_groups * G_BUCK).astype(jnp.int32)
    bucket_centres = top_centres(bucket_top)
    cell_centres = top_centres(jnp.arange(TOP, dtype=jnp.int32))
    places = positions
    speeds = velocities
    accel_now = accel_prev
    for substep in range(STEPS):
        half_speed = speeds + 0.5 * time_step * activity * accel_now
        places = places + time_step * half_speed
        bucketed = places.reshape(3, NBUCK, BUCKET)
        bucket_mass = masses.reshape(NBUCK, BUCKET)
        bucket_cells = bucket_moments(bucketed, bucket_mass)
        per_bucket = top_raw(bucketed, bucket_mass, bucket_centres)
        summed = jax.ops.segment_sum(per_bucket.T, bucket_top, num_segments=TOP).T
        top_cells = top_moments(summed, cell_centres)

        def one_bucket(work_item):
            global_id, group_id = work_item
            near_ids = (near_list[global_id] + group_id * G_BUCK).astype(jnp.int32)
            cell_ids = essential_ids[group_id][cell_list[global_id]]
            return force_one(bucketed[:, global_id], near_ids, cell_ids, top_list[global_id], bucketed, bucket_mass, bucket_cells, top_cells)
        forces = in_blocks(one_bucket, (work_global, work_groups), N_DOM * N_SUB * W_DEV)
        spread_forces = jnp.zeros((3, NBUCK, BUCKET), jnp.float32).at[:, work_global].set(jnp.transpose(forces, (1, 0, 2)))
        accel_now = spread_forces.reshape(3, NPART)
        speeds = half_speed + 0.5 * time_step * activity * accel_now
    return (speeds, places)
```

```python
import functools

import jax
import jax.numpy as jnp
from jax import lax
from jax.experimental import pallas as pl
from jax.experimental.pallas import tpu as pltpu
from jax.sharding import PartitionSpec as P

TOP_SIDE = 16
TOP = TOP_SIDE**3
DT = 0.01
EPS = 0.0025
MASS_FLOOR = 0.5
LANES = 128
ROWS = 16


f32 = jnp.float32
bf16 = jnp.bfloat16


def other_slot(index, size, me):
    if size & (size - 1) == 0:
        return index ^ (me * size)
    return ((index // size) ^ me) * size + index % size


def to_tiles(three, one):
    flat = jnp.concatenate([three, one[None]], axis=0)
    count = flat.shape[1] // (2 * LANES)
    return flat.reshape(4, count, 2, LANES).transpose(1, 2, 0, 3).reshape(count, 8, LANES)


def from_tiles(tiles):
    count = tiles.shape[0]
    flat = tiles.reshape(count, 2, 4, LANES).transpose(2, 0, 1, 3).reshape(4, count * 2 * LANES)
    return flat[:3]


def sub_gather(block, sub_count):
    parts = [None] * sub_count
    parts[0] = block
    for step in range(0, sub_count, 2):
        if step:
            parts[step] = lax.ppermute(block, "sub", [(i, i ^ step) for i in range(sub_count)])
    for step in range(0, sub_count, 2):
        parts[step + 1] = lax.ppermute(
            parts[step], "sub", [(i, i ^ 1) for i in range(sub_count)]
        )
    return parts


def row_iota(shape=(8, LANES)):
    return lax.broadcasted_iota(jnp.int32, shape, 0)


def rounded(values):
    return values.astype(bf16).astype(f32)


def moments_of(get, bucket_count):
    weights = [get(0, 3), get(1, 3)]
    places = [[get(half, axis) for axis in range(3)] for half in range(2)]

    def total(one, two):
        return jnp.sum(one + two, axis=1, keepdims=True)

    mass = total(weights[0], weights[1])
    centre = [
        total(weights[0] * places[0][axis], weights[1] * places[1][axis]) / mass
        for axis in range(3)
    ]
    off = [[places[half][axis] - centre[axis] for axis in range(3)] for half in range(2)]
    woff = [[weights[half] * off[half][axis] for axis in range(3)] for half in range(2)]

    def second(a, b):
        return total(woff[0][a] * off[0][b], woff[1][a] * off[1][b])

    xx, yy, zz = second(0, 0), second(1, 1), second(2, 2)
    trace = xx + yy + zz
    return [mass] + centre + [
        3.0 * xx - trace,
        3.0 * yy - trace,
        3.0 * zz - trace,
        3.0 * second(0, 1),
        3.0 * second(0, 2),
        3.0 * second(1, 2),
    ]


def write_moments(columns, tops_row, out_ref, bucket_count):
    lane = lax.broadcasted_iota(jnp.int32, (bucket_count, LANES), 1)
    wide = jnp.zeros((bucket_count, LANES), f32)
    for q, column in enumerate(columns):
        wide = jnp.where(lane == q, column, wide)
    turned = jnp.transpose(wide)
    for block in range(bucket_count // LANES):
        rows = turned[:ROWS, block * LANES : (block + 1) * LANES]
        sub = lax.broadcasted_iota(jnp.int32, (ROWS, LANES), 0)
        rows = jnp.where(sub == 10, tops_row[:, block * LANES : (block + 1) * LANES], rows)
        out_ref[block] = rows


def first_moments_kernel(tiles_ref, tops_ref, out_ref):
    bucket_count = tiles_ref.shape[0]
    columns = moments_of(lambda half, row: tiles_ref[:, 4 * half + row, :], bucket_count)
    write_moments(columns, tops_ref[...], out_ref, bucket_count)


def spread_own(acc_ref, work_ref, me, own_ref, bucket_count):
    own_ref[...] = jnp.zeros_like(own_ref)
    for part in range(work_ref.shape[0]):

        @pl.loop(0, work_ref.shape[1])
        def _(i):
            bucket = work_ref[part, i]
            mine = bucket // bucket_count == me
            slot = jnp.where(mine, bucket % bucket_count, bucket_count)
            own_ref[slot] = acc_ref[part, i]


def second_moments_kernel(
    me_ref, work_ref, ahead_ref, tiles_ref, acc_ref, tops_ref, out_ref, places_ref, own_ref
):
    bucket_count = tiles_ref.shape[0]
    spread_own(acc_ref, work_ref, me_ref[0], own_ref, bucket_count)
    for half in range(2):
        act = ahead_ref[:, 4 * half + 3, :] * (DT * DT)
        for axis in range(3):
            row = 4 * half + axis
            places_ref[:, row, :] = ahead_ref[:, row, :] + act * own_ref[:bucket_count, row, :]
        places_ref[:, 4 * half + 3, :] = tiles_ref[:, 4 * half + 3, :]
    columns = moments_of(lambda half, row: places_ref[:, 4 * half + row, :], bucket_count)
    write_moments(columns, tops_ref[...], out_ref, bucket_count)


def final_kernel(me_ref, work_ref, ahead_ref, half_ref, acc_one_ref, acc_two_ref, out_ref, one_ref, two_ref):
    bucket_count = ahead_ref.shape[0]
    spread_own(acc_one_ref, work_ref, me_ref[0], one_ref, bucket_count)
    spread_own(acc_two_ref, work_ref, me_ref[0], two_ref, bucket_count)
    for half in range(2):
        act = ahead_ref[:, 4 * half + 3, :]
        for axis in range(3):
            row = 4 * half + axis
            out_ref[:, row, :] = half_ref[:, row, :] + act * (
                DT * one_ref[:bucket_count, row, :] + 0.5 * DT * two_ref[:bucket_count, row, :]
            )
        out_ref[:, 4 * half + 3, :] = act


def traceless(diag, cross):
    trace = diag[0] + diag[1] + diag[2]
    return [3.0 * d - trace for d in diag] + [3.0 * c for c in cross]


def outer(first, second):
    return (
        [first[a] * second[a] for a in range(3)],
        [first[0] * second[1], first[0] * second[2], first[1] * second[2]],
    )


def build_rows(cells_ref, rows_ref, raw_ref, raw_low_ref, sums_ref, tops_ref):
    blocks = cells_ref.shape[0]
    top_blocks = TOP // LANES
    for block in range(blocks):
        rows_ref[block * LANES : (block + 1) * LANES, :ROWS] = jnp.transpose(cells_ref[block])
    side = TOP_SIDE
    top_id = cells_ref[:, 10, :].astype(jnp.int32)
    index = [top_id // (side * side), top_id // side % side, top_id % side]
    mass = cells_ref[:, 0, :]
    delta = [cells_ref[:, 1 + a, :] - (index[a].astype(f32) + 0.5) / side for a in range(3)]
    first = [mass * delta[a] for a in range(3)]
    lifted = traceless(*outer(first, delta))
    raw = [mass] + first + [cells_ref[:, 4 + k, :] + lifted[k] for k in range(6)]
    zero = jnp.zeros_like(mass)
    for q in range(ROWS):
        value = raw[q] if q < 10 else zero
        raw_ref[:, q, :] = rounded(value)
        raw_low_ref[:, q, :] = value - rounded(value)
    sums_ref[...] = jnp.zeros_like(sums_ref)
    pair = 2 if blocks % 2 == 0 else 1

    @pl.loop(0, blocks // pair)
    def _(step):
        wide_top, wide_high, wide_low = [], [], []
        for part in range(pair):
            block = step * pair + part
            wide_top.append(cells_ref[block][10:11, :])
            wide_high.append(raw_ref[block])
            wide_low.append(raw_low_ref[block])
        top = jnp.concatenate(wide_top, axis=1).astype(jnp.int32)
        high = jnp.concatenate(wide_high, axis=1).astype(bf16)
        low = jnp.concatenate(wide_low, axis=1).astype(bf16)
        width = top.shape[1]
        upper = jnp.broadcast_to(top // LANES, (ROWS, width))
        lower = top % LANES
        match = (
            lax.broadcasted_iota(jnp.int32, (LANES, width), 0) == jnp.broadcast_to(lower, (LANES, width))
        )
        picks = jnp.where(match, 1.0, 0.0).astype(bf16)
        empty = jnp.zeros_like(high)
        left = []
        for values in (high, low):
            left.append(
                jnp.concatenate(
                    [jnp.where(upper == u, values, empty) for u in range(top_blocks)], axis=0
                )
            )
        both = lax.dot_general(
            left[0], picks, (((1,), (1,)), ((), ())), preferred_element_type=f32
        ) + lax.dot_general(left[1], picks, (((1,), (1,)), ((), ())), preferred_element_type=f32)
        sums_ref[...] += both.reshape(sums_ref.shape)

    upper = lax.broadcasted_iota(jnp.int32, (top_blocks, LANES), 0)
    lower = lax.broadcasted_iota(jnp.int32, (top_blocks, LANES), 1)
    cell = upper * LANES + lower
    index = [cell // (side * side), cell // side % side, cell % side]
    mass = sums_ref[:, 0, :]
    safe = jnp.maximum(mass, MASS_FLOOR)
    first = [sums_ref[:, 1 + a, :] for a in range(3)]
    shift = [first[a] / safe for a in range(3)]
    lowered = traceless(*outer(first, shift))
    tops_ref[:, 0, :] = mass
    for a in range(3):
        tops_ref[:, 1 + a, :] = (index[a].astype(f32) + 0.5) / side + shift[a]
    for k in range(6):
        tops_ref[:, 4 + k, :] = sums_ref[:, 4 + k, :] - lowered[k]
    for q in range(10, ROWS):
        tops_ref[:, q, :] = jnp.zeros_like(mass)
    for block in range(top_blocks):
        start = (blocks + block) * LANES
        rows_ref[start : start + LANES, :ROWS] = jnp.transpose(tops_ref[block])


def cell_sum(cells, tile):
    count = cells.shape[0]
    places = [
        [jnp.broadcast_to(tile[4 * half + a : 4 * half + a + 1, :], (8, LANES)) for a in range(3)]
        for half in range(2)
    ]
    sums = [[jnp.zeros((8, LANES), f32) for _ in range(3)] for _ in range(2)]
    for group in range(count // 8):
        block = cells[8 * group : 8 * group + 8, :]
        column = [jnp.broadcast_to(block[:, q : q + 1], (8, LANES)) for q in range(10)]
        for half in range(2):
            off = [places[half][a] - column[1 + a] for a in range(3)]
            dist = off[0] * off[0] + off[1] * off[1] + off[2] * off[2] + EPS
            inv = lax.rsqrt(dist)
            inv_two = inv * inv
            inv_five = inv_two * inv_two * inv
            along = [
                column[4] * off[0] + column[7] * off[1] + column[8] * off[2],
                column[7] * off[0] + column[5] * off[1] + column[9] * off[2],
                column[8] * off[0] + column[9] * off[1] + column[6] * off[2],
            ]
            both = off[0] * along[0] + off[1] * along[1] + off[2] * along[2]
            radial = column[0] * dist + 2.5 * both * inv_two
            for a in range(3):
                sums[half][a] += (along[a] - radial * off[a]) * inv_five
    row = row_iota()
    result = jnp.zeros((8, LANES), f32)
    for half in range(2):
        for a in range(3):
            value = jnp.sum(sums[half][a], axis=0, keepdims=True)
            result = jnp.where(row == 4 * half + a, jnp.broadcast_to(value, (8, LANES)), result)
    return result


def near_sum(tile, sources):
    row = row_iota()
    last = row % 4 == 3
    front = row < 4
    mean = jnp.sum(tile, axis=1, keepdims=True)
    mean = jnp.broadcast_to(mean, (8, LANES))
    centre = jnp.where(last, 0.0, (mean + pltpu.roll(mean, 4, 0)) * (0.5 / LANES))

    def with_norm(values, extra, scale):
        squares = jnp.where(last, 0.0, values * values)
        norm = pltpu.roll(squares, 1, 0) + pltpu.roll(squares, 2, 0) + pltpu.roll(squares, 3, 0)
        return jnp.where(last, norm + extra, scale * values)

    def three(values):
        high = rounded(values)
        rest = values - high
        middle = rounded(rest)
        return high, middle, rest - middle

    target = tile - centre
    high, middle, low = three(with_norm(target, EPS, -2.0))
    plain = jnp.where(last, 1.0, high)
    blocks = [plain, plain, plain, jnp.where(last, high, middle), middle, low]
    turned = [pltpu.roll(block, 4, 0) for block in blocks]
    left = jnp.concatenate(
        [
            jnp.transpose(jnp.concatenate([jnp.where(front, b, t) for b, t in zip(blocks, turned)], axis=0)),
            jnp.transpose(jnp.concatenate([jnp.where(front, t, b) for b, t in zip(blocks, turned)], axis=0)),
        ],
        axis=0,
    ).astype(bf16)
    total = jnp.zeros((32, 2 * LANES), f32)
    for source in sources:
        place = source - centre
        high, middle, low = three(with_norm(place, 0.0, 1.0))
        high_one = jnp.where(last, 1.0, high)
        middle_one = jnp.where(last, 1.0, middle)
        blocks = [high, middle, low, high_one, middle_one, high_one]
        right = jnp.concatenate(
            [
                jnp.concatenate([jnp.where(front, b, 0.0) for b in blocks], axis=0),
                jnp.concatenate([jnp.where(front, 0.0, b) for b in blocks], axis=0),
            ],
            axis=1,
        ).astype(bf16)
        dist = jnp.dot(left, right, preferred_element_type=f32)
        inv = lax.rsqrt(dist)
        weight = (inv * inv * inv).astype(bf16)
        mass = jnp.where(last, source, 0.0)
        mass = mass + pltpu.roll(mass, 7, 0) + pltpu.roll(mass, 6, 0) + pltpu.roll(mass, 5, 0)
        moved = mass * place
        moved_high, mass_high = rounded(moved), rounded(mass)
        blocks = [moved_high, moved - moved_high, mass_high, mass - mass_high]
        pulls = jnp.concatenate(
            [
                jnp.concatenate([jnp.where(front, b, 0.0) for b in blocks], axis=0),
                jnp.concatenate([jnp.where(front, 0.0, b) for b in blocks], axis=0),
            ],
            axis=1,
        ).astype(bf16)
        total += lax.dot_general(
            pulls, weight, (((1,), (1,)), ((), ())), preferred_element_type=f32
        )
    moved = total[0:8] + total[8:16]
    mass = total[16:24] + total[24:32]

    def fold(values):
        one, two = values[:, :LANES], values[:, LANES:]
        return jnp.where(front, one + pltpu.roll(one, 4, 0), two + pltpu.roll(two, 4, 0))

    return jnp.where(last, 0.0, fold(moved) - target * fold(mass))


def force_kernel(
    second,
    sub_count,
    bucket_count,
    near_count,
    cell_count,
    top_count,
    me_ref,
    work_ref,
    list_ref,
    ess_ref,
    *refs,
):
    refs = list(refs)
    cells_ref = refs.pop(0)
    table_refs = [refs.pop(0) for _ in range(sub_count)]
    if second:
        mass_refs = [refs.pop(0) for _ in range(sub_count)]
        acc_ref = refs.pop(0)
    out_ref = refs.pop(0)
    group_ref, rows_ref, raw_ref, raw_low_ref, sums_ref, tops_ref, picked_ref, sem = refs[:8]
    me = me_ref[0]
    copies = [
        pltpu.make_async_copy(
            table_refs[k], group_ref.at[pl.ds(k * bucket_count, bucket_count)], sem.at[k]
        )
        for k in range(sub_count)
    ]
    for copy in copies:
        copy.start()
    if second:
        base_ref = refs[8]
        others = [
            pltpu.make_async_copy(
                mass_refs[k],
                base_ref.at[pl.ds(k * bucket_count, bucket_count)],
                sem.at[sub_count + k],
            )
            for k in range(sub_count)
        ]
        for copy in others:
            copy.start()
    build_rows(cells_ref, rows_ref, raw_ref, raw_low_ref, sums_ref, tops_ref)
    for copy in copies:
        copy.wait()
    row = row_iota()
    last = row % 4 == 3
    if second:
        for copy in others:
            copy.wait()
        for part in range(sub_count):

            @pl.loop(0, work_ref.shape[1])
            def _(i):
                slot = other_slot(work_ref[part, i], bucket_count, me)
                tile = group_ref[slot]
                act = jnp.where(last, tile, 0.0)
                act = act + pltpu.roll(act, 7, 0) + pltpu.roll(act, 6, 0) + pltpu.roll(act, 5, 0)
                group_ref[slot] = tile + (DT * DT) * act * acc_ref[part, i]

        @pl.loop(0, sub_count * bucket_count // 8)
        def _(i):
            at = pl.ds(i * 8, 8)
            wide = lax.broadcasted_iota(jnp.int32, (8, 8, LANES), 1) % 4 == 3
            group_ref[at] = jnp.where(wide, base_ref[at], group_ref[at])

    ess_size = ess_ref.shape[0] // sub_count
    first_top = cells_ref.shape[0] * LANES

    @pl.loop(0, work_ref.shape[1])
    def _(i):
        for k in range(cell_count):
            bucket = ess_ref[other_slot(list_ref[i, near_count + k], ess_size, me)]
            picked_ref[pl.ds(k, 1), :] = rows_ref[pl.ds(bucket, 1), :]
        for k in range(top_count):
            top = first_top + list_ref[i, near_count + cell_count + k]
            picked_ref[pl.ds(cell_count + k, 1), :] = rows_ref[pl.ds(top, 1), :]
        tile = group_ref[other_slot(work_ref[0, i], bucket_count, me)]
        sources = [
            group_ref[other_slot(list_ref[i, k], bucket_count, me)] for k in range(near_count)
        ]
        out_ref[i] = near_sum(tile, sources) + cell_sum(picked_ref, tile)


def body(
    positions,
    velocities,
    masses,
    accel_prev,
    active,
    bucket_top,
    near_list,
    cell_list,
    top_list,
    essential,
    work,
):
    bucket_count = bucket_top.shape[0]
    sub_count = lax.axis_size("sub")
    dom_count = lax.axis_size("dom")
    me = lax.axis_index("sub").astype(jnp.int32)
    group_buckets = sub_count * bucket_count
    device_count = sub_count * dom_count
    near_count, cell_count, top_count = near_list.shape[1], cell_list.shape[1], top_list.shape[1]
    work_count = work.shape[0]
    vmem = pl.BlockSpec(memory_space=pltpu.VMEM)
    smem = pl.BlockSpec(memory_space=pltpu.SMEM)
    anywhere = pl.BlockSpec(memory_space=pl.ANY)
    tile_shape = jax.ShapeDtypeStruct((bucket_count, 8, LANES), f32)
    moment_shape = jax.ShapeDtypeStruct((bucket_count // LANES, ROWS, LANES), f32)

    activity = active.astype(f32)
    half_speed = velocities + 0.5 * DT * activity * accel_prev
    places = positions + DT * half_speed
    tiles = to_tiles(places, masses)
    ahead = to_tiles(places + DT * half_speed, activity)
    speeds = to_tiles(half_speed, activity)

    lists = jnp.concatenate([near_list, cell_list, top_list], axis=1)
    lists = jnp.pad(lists, ((0, 0), (0, -lists.shape[1] % LANES)))
    wanted = essential.reshape(dom_count, -1) + (
        jnp.arange(dom_count, dtype=jnp.int32) * group_buckets
    )[:, None]
    wanted = wanted.reshape(-1)
    extra = jnp.concatenate([wanted, work])
    extra = jnp.pad(extra, (0, -extra.shape[0] % LANES))
    sent = jnp.concatenate([lists.reshape(-1), extra])
    tops_row = bucket_top.astype(f32)[None]

    list_parts = sub_gather(sent, sub_count)
    table = sub_gather(tiles, sub_count)
    table_ahead = sub_gather(ahead, sub_count)

    width = lists.shape[1]
    list_table = jnp.stack(
        [part[: bucket_count * width].reshape(bucket_count, width) for part in list_parts]
    ).reshape(group_buckets, width)
    ess_all = jnp.concatenate(
        [part[bucket_count * width :][: wanted.shape[0]] for part in list_parts]
    )
    work_all = jnp.stack(
        [
            part[bucket_count * width + wanted.shape[0] :][:work_count]
            for part in list_parts
        ]
    )
    work_lists = jnp.take(list_table, other_slot(work, bucket_count, me), axis=0)
    me_one = me[None]

    def exchange(own):
        wide = jnp.broadcast_to(own.reshape(1, -1), (device_count, own.size))
        got = lax.all_to_all(wide, ("dom", "sub"), split_axis=0, concat_axis=0, tiled=True)
        return got.reshape(-1, ROWS, LANES)

    def force(second, cells, tables, extra_tables):
        blocks = cells.shape[0]
        scratch = [
            pltpu.VMEM((group_buckets, 8, LANES), f32),
            pltpu.VMEM((blocks * LANES + TOP, LANES), f32),
            pltpu.VMEM((blocks, ROWS, LANES), f32),
            pltpu.VMEM((blocks, ROWS, LANES), f32),
            pltpu.VMEM((TOP // LANES, ROWS, LANES), f32),
            pltpu.VMEM((TOP // LANES, ROWS, LANES), f32),
            pltpu.VMEM((cell_count + top_count, LANES), f32),
            pltpu.SemaphoreType.DMA((2 * sub_count,)),
        ]
        specs = [smem] * 4 + [vmem] + [anywhere] * sub_count
        if second:
            specs += [anywhere] * sub_count + [vmem]
            scratch.append(pltpu.VMEM((group_buckets, 8, LANES), f32))
        kernel = functools.partial(
            force_kernel, second, sub_count, bucket_count, near_count, cell_count, top_count
        )
        return pl.pallas_call(
            kernel,
            out_shape=jax.ShapeDtypeStruct((work_count, 8, LANES), f32),
            in_specs=specs,
            out_specs=vmem,
            scratch_shapes=scratch,
            name="force_second" if second else "force_first",
        )(me_one, work_all, work_lists, ess_all, cells, *tables, *extra_tables)

    cells = exchange(
        pl.pallas_call(
            first_moments_kernel,
            out_shape=moment_shape,
            in_specs=[vmem] * 2,
            out_specs=vmem,
            name="first_moments",
        )(tiles, tops_row)
    )
    acc_one = jnp.stack(sub_gather(force(False, cells, table, []), sub_count))
    own_scratch = pltpu.VMEM((bucket_count + 1, 8, LANES), f32)
    own_moments, places_two = pl.pallas_call(
        second_moments_kernel,
        out_shape=(moment_shape, tile_shape),
        in_specs=[smem] * 2 + [vmem] * 4,
        out_specs=(vmem, vmem),
        scratch_shapes=[own_scratch],
        name="second_moments",
    )(me_one, work_all, ahead, tiles, acc_one, tops_row)
    cells = exchange(own_moments)
    acc_two = jnp.stack(
        sub_gather(force(True, cells, table_ahead, [*table, acc_one]), sub_count)
    )
    speed_two = pl.pallas_call(
        final_kernel,
        out_shape=tile_shape,
        in_specs=[smem] * 2 + [vmem] * 4,
        out_specs=vmem,
        scratch_shapes=[own_scratch] * 2,
        name="final_speeds",
    )(me_one, work_all, ahead, speeds, acc_one, acc_two)
    return from_tiles(speed_two), from_tiles(places_two)


def solution(mesh):
    both = ("dom", "sub")
    in_specs = (
        P(None, both),
        P(None, both),
        P(both),
        P(None, both),
        P(both),
        P(both),
        P(both, None),
        P(both, None),
        P(both, None),
        P("dom", "sub", None, None),
        P(both),
    )
    out_specs = (P(None, both), P(None, both))
    return jax.shard_map(body, mesh=mesh, in_specs=in_specs, out_specs=out_specs, check_vma=False)
```

```python
import functools

import jax
import jax.numpy as jnp
from jax import lax
from jax.experimental import pallas as pl
from jax.experimental.pallas import tpu as pltpu
from jax.sharding import PartitionSpec as P

TOP_SIDE = 16
TOP = TOP_SIDE**3
DT = 0.01
EPS = 0.0025
MASS_FLOOR = 0.5
LANES = 128
ROWS = 16
SENT = 11
LOWER = 256
PARTS = 4 * ROWS
CELL_CHUNK = 32
CELL_SPAN = 4


f32 = jnp.float32
bf16 = jnp.bfloat16


def other_slot(index, size, me):
    if size & (size - 1) == 0:
        return index ^ (me * size)
    return ((index // size) ^ me) * size + index % size


def to_tiles(three, one):
    flat = jnp.concatenate([three, one[None]], axis=0)
    count = flat.shape[1] // (2 * LANES)
    return flat.reshape(4, count, 2, LANES).transpose(1, 2, 0, 3).reshape(count, 8, LANES)


def from_tiles(tiles):
    count = tiles.shape[0]
    flat = tiles.reshape(count, 2, 4, LANES).transpose(2, 0, 1, 3).reshape(4, count * 2 * LANES)
    return flat[:3]


def sub_gather(block, sub_count):
    parts = [None] * sub_count
    parts[0] = block
    for step in range(0, sub_count, 2):
        if step:
            parts[step] = lax.ppermute(block, "sub", [(i, i ^ step) for i in range(sub_count)])
    for step in range(0, sub_count, 2):
        parts[step + 1] = lax.ppermute(
            parts[step], "sub", [(i, i ^ 1) for i in range(sub_count)]
        )
    return parts


def row_iota(shape=(8, LANES)):
    return lax.broadcasted_iota(jnp.int32, shape, 0)


def rounded(values):
    return values.astype(bf16).astype(f32)


def moments_of(get, bucket_count):
    weights = [get(0, 3), get(1, 3)]
    places = [[get(half, axis) for axis in range(3)] for half in range(2)]

    def total(one, two):
        return jnp.sum(one + two, axis=1, keepdims=True)

    mass = total(weights[0], weights[1])
    centre = [
        total(weights[0] * places[0][axis], weights[1] * places[1][axis]) / mass
        for axis in range(3)
    ]
    off = [[places[half][axis] - centre[axis] for axis in range(3)] for half in range(2)]
    woff = [[weights[half] * off[half][axis] for axis in range(3)] for half in range(2)]

    def second(a, b):
        return total(woff[0][a] * off[0][b], woff[1][a] * off[1][b])

    xx, yy, zz = second(0, 0), second(1, 1), second(2, 2)
    trace = xx + yy + zz
    return [mass] + centre + [
        3.0 * xx - trace,
        3.0 * yy - trace,
        3.0 * zz - trace,
        3.0 * second(0, 1),
        3.0 * second(0, 2),
        3.0 * second(1, 2),
    ]


def write_moments(columns, tops_row, out_ref, bucket_count):
    lane = lax.broadcasted_iota(jnp.int32, (bucket_count, LANES), 1)
    wide = jnp.zeros((bucket_count, LANES), f32)
    for q, column in enumerate(columns):
        wide = jnp.where(lane == q, column, wide)
    turned = jnp.transpose(wide)
    blocks = bucket_count // LANES
    for block in range(blocks):
        at = slice(block * LANES, (block + 1) * LANES)
        rows = jnp.concatenate([turned[:10, at], tops_row[:, at]], axis=0)
        for copy in range(out_ref.shape[0] // (blocks * SENT)):
            start = (copy * blocks + block) * SENT
            out_ref[start : start + SENT, :] = rows


def tile_rows(ref, row, bucket_count):
    return ref[pl.ds(row, bucket_count, stride=8), :]


def first_moments_kernel(tiles_ref, tops_ref, out_ref):
    bucket_count = tiles_ref.shape[0] // 8
    columns = moments_of(
        lambda half, row: tile_rows(tiles_ref, 4 * half + row, bucket_count), bucket_count
    )
    write_moments(columns, tops_ref[...], out_ref, bucket_count)


def spread_own(acc_refs, work_ref, me, own_ref, bucket_count):
    own_ref[...] = jnp.zeros_like(own_ref)
    count = work_ref.shape[1]
    for part, acc_ref in enumerate(acc_refs):

        @pl.loop(0, count, unroll=8 if count % 8 == 0 else 1)
        def _(i):
            bucket = work_ref[part, i] - me * bucket_count
            mine = jnp.logical_and(bucket >= 0, bucket < bucket_count)
            slot = pl.multiple_of(jnp.where(mine, bucket, bucket_count) * 8, 8)
            own_ref[pl.ds(slot, 8), :] = acc_ref[i]


def act_rows(tiles):
    count = tiles.shape[0] // 8
    wide = tiles.reshape(count, 8, LANES)
    row = lax.broadcasted_iota(jnp.int32, wide.shape, 1)
    first = jnp.broadcast_to(wide[:, 3:4, :], wide.shape)
    second = jnp.broadcast_to(wide[:, 7:8, :], wide.shape)
    return row % 4 == 3, jnp.where(row < 4, first, second), wide


def second_moments_kernel(sub_count, me_ref, work_ref, ahead_ref, tiles_ref, tops_ref, *refs):
    acc_refs, (out_ref, places_ref, own_ref) = refs[:sub_count], refs[sub_count:]
    bucket_count = tiles_ref.shape[0] // 8
    spread_own(acc_refs, work_ref, me_ref[0], own_ref, bucket_count)

    @pl.loop(0, bucket_count // 8)
    def _(i):
        at = pl.ds(pl.multiple_of(i * 64, 64), 64)
        last, act, ahead = act_rows(ahead_ref[at, :])
        moved = ahead + (DT * DT) * act * own_ref[at, :].reshape(8, 8, LANES)
        places = jnp.where(last, tiles_ref[at, :].reshape(8, 8, LANES), moved)
        places_ref[at, :] = places.reshape(64, LANES)

    columns = moments_of(
        lambda half, row: tile_rows(places_ref, 4 * half + row, bucket_count), bucket_count
    )
    write_moments(columns, tops_ref[...], out_ref, bucket_count)


def final_kernel(sub_count, me_ref, work_ref, speeds_ref, own_one_ref, *refs):
    acc_refs, (out_ref, two_ref) = refs[:sub_count], refs[sub_count:]
    bucket_count = speeds_ref.shape[0] // 8
    spread_own(acc_refs, work_ref, me_ref[0], two_ref, bucket_count)

    @pl.loop(0, bucket_count // 8)
    def _(i):
        at = pl.ds(pl.multiple_of(i * 64, 64), 64)
        _, act, speeds = act_rows(speeds_ref[at, :])
        one = own_one_ref[at, :].reshape(8, 8, LANES)
        two = two_ref[at, :].reshape(8, 8, LANES)
        out_ref[at, :] = (speeds + act * (DT * one + 0.5 * DT * two)).reshape(64, LANES)


def traceless(diag, cross):
    trace = diag[0] + diag[1] + diag[2]
    return [3.0 * d - trace for d in diag] + [3.0 * c for c in cross]


def outer(first, second):
    return (
        [first[a] * second[a] for a in range(3)],
        [first[0] * second[1], first[0] * second[2], first[1] * second[2]],
    )


def in_parts(values):
    high, middle, low = three(values)
    return jnp.concatenate([high, middle, low, jnp.ones_like(values)], axis=0)


def build_rows(cells_ref, rows_ref, raw_ref, sums_ref, tops_ref):
    blocks = cells_ref.shape[0] // SENT
    uppers = TOP // LOWER
    for block in range(blocks):
        start = block * SENT
        if start + ROWS <= cells_ref.shape[0]:
            turned = cells_ref[start : start + ROWS, :]
        else:
            turned = jnp.concatenate(
                [cells_ref[start : start + SENT, :], jnp.zeros((ROWS - SENT, LANES), f32)], axis=0
            )
        rows_ref[block * LANES : (block + 1) * LANES, :PARTS] = jnp.transpose(in_parts(turned))
    side = TOP_SIDE

    def sent(q):
        return cells_ref[pl.ds(q, blocks, stride=SENT), :]

    top_id = sent(10).astype(jnp.int32)
    index = [top_id // (side * side), top_id // side % side, top_id % side]
    mass = sent(0)
    delta = [sent(1 + a) - (index[a].astype(f32) + 0.5) / side for a in range(3)]
    first = [mass * delta[a] for a in range(3)]
    lifted = traceless(*outer(first, delta))
    raw = [mass] + first + [sent(4 + k) + lifted[k] for k in range(6)]
    for q in range(ROWS):
        raw_ref[q * blocks : (q + 1) * blocks, :] = raw[q] if q < 10 else jnp.zeros_like(mass)
    sums_ref[...] = jnp.zeros_like(sums_ref)
    pair = 2 if blocks % 2 == 0 else 1

    @pl.loop(0, blocks // pair)
    def _(step):
        top, values = [], []
        for part in range(pair):
            block = step * pair + part
            top.append(cells_ref[pl.ds(block * SENT + 10, 1), :])
            values.append(raw_ref[pl.ds(block, ROWS, stride=blocks), :])
        top = jnp.concatenate(top, axis=1).astype(jnp.int32)
        values = jnp.concatenate(values, axis=1)
        high = values.astype(bf16)
        low = (values - high.astype(f32)).astype(bf16)
        width = top.shape[1]
        upper = jnp.broadcast_to(top // LOWER, (ROWS, width))
        lower = jnp.broadcast_to(top % LOWER, (LOWER, width))
        match = lax.broadcasted_iota(jnp.int32, (LOWER, width), 0) == lower
        picks = jnp.where(match, 1.0, 0.0).astype(bf16)
        empty = jnp.zeros_like(high)
        parts = []
        for piece in (high, low):
            left = jnp.concatenate(
                [jnp.where(upper == u, piece, empty) for u in range(uppers)], axis=0
            )
            parts.append(
                lax.dot_general(left, picks, (((1,), (1,)), ((), ())), preferred_element_type=f32)
            )
        sums_ref[...] += parts[0] + parts[1]

    cell = lax.broadcasted_iota(jnp.int32, (uppers, LOWER), 0) * LOWER
    cell = cell + lax.broadcasted_iota(jnp.int32, (uppers, LOWER), 1)
    index = [cell // (side * side), cell // side % side, cell % side]

    def summed(q):
        return jnp.concatenate(
            [sums_ref[u * ROWS + q : u * ROWS + q + 1, :] for u in range(uppers)], axis=0
        )

    mass = summed(0)
    inverse = 1.0 / jnp.maximum(mass, MASS_FLOOR)
    first = [summed(1 + a) for a in range(3)]
    shift = [first[a] * inverse for a in range(3)]
    lowered = traceless(*outer(first, shift))
    tops = (
        [mass]
        + [(index[a].astype(f32) + 0.5) / side + shift[a] for a in range(3)]
        + [summed(4 + k) - lowered[k] for k in range(6)]
    )
    for q in range(10):
        for u in range(uppers):
            tops_ref[u * ROWS + q : u * ROWS + q + 1, :] = tops[q][u : u + 1, :]
    for u in range(uppers):
        start = blocks * LANES + u * LOWER
        rows_ref[start : start + LOWER, :PARTS] = jnp.transpose(
            in_parts(tops_ref[u * ROWS : (u + 1) * ROWS, :])
        )


def cell_terms(off, mass, quad, sums):
    dist = off[0] * off[0] + off[1] * off[1] + off[2] * off[2] + EPS
    inv = lax.rsqrt(dist)
    inv_two = inv * inv
    inv_five = inv_two * inv_two * inv
    along = [
        quad[0] * off[0] + quad[3] * off[1] + quad[4] * off[2],
        quad[3] * off[0] + quad[1] * off[1] + quad[5] * off[2],
        quad[4] * off[0] + quad[5] * off[1] + quad[2] * off[2],
    ]
    both = off[0] * along[0] + off[1] * along[1] + off[2] * along[2]
    radial = mass * dist + 2.5 * both * inv_two
    for a in range(3):
        sums[a] += (along[a] - radial * off[a]) * inv_five


def with_norm(values, extra, scale, last):
    squares = jnp.where(last, 0.0, values * values)
    norm = pltpu.roll(squares, 1, 0) + pltpu.roll(squares, 2, 0) + pltpu.roll(squares, 3, 0)
    return jnp.where(last, norm + extra, scale * values)


def three(values):
    high = rounded(values)
    rest = values - high
    middle = rounded(rest)
    return high, middle, rest - middle


def prepare_near(tile, sources, left_ref, right_ref, pull_ref, target_ref):
    row = row_iota()
    last = row % 4 == 3
    front = row < 4
    mean = jnp.sum(tile, axis=1, keepdims=True)
    mean = jnp.broadcast_to(mean, (8, LANES))
    centre = jnp.where(last, 0.0, (mean + pltpu.roll(mean, 4, 0)) * (0.5 / LANES))
    target = tile - centre
    target_ref[...] = target
    high, middle, low = three(with_norm(target, EPS, -2.0, last))
    plain = jnp.where(last, 1.0, high)
    blocks = [plain, plain, plain, jnp.where(last, high, middle), middle, low]
    turned = [pltpu.roll(block, 4, 0) for block in blocks]
    first = [jnp.where(front, b, t) for b, t in zip(blocks, turned)]
    second = [jnp.where(front, t, b) for b, t in zip(blocks, turned)]
    for half in range(2):
        keep = front if half == 0 else jnp.logical_not(front)
        for side, parts in enumerate((first, second)):
            right_ref[half, :, side * LANES : (side + 1) * LANES] = jnp.concatenate(
                [jnp.where(keep, part, 0.0) for part in parts], axis=0
            ).astype(bf16)
    for k, source in enumerate(sources):
        at = slice(k * LANES, (k + 1) * LANES)
        place = source - centre
        high, middle, low = three(with_norm(place, 0.0, 1.0, last))
        high_one = jnp.where(last, 1.0, high)
        middle_one = jnp.where(last, 1.0, middle)
        stack = jnp.concatenate([high, middle, low, high_one, middle_one, high_one], axis=0)
        left_ref[at, :] = jnp.transpose(stack).astype(bf16)
        mass = jnp.where(last, source, 0.0)
        mass = mass + pltpu.roll(mass, 7, 0) + pltpu.roll(mass, 6, 0) + pltpu.roll(mass, 5, 0)
        moved = mass * place
        moved_high, mass_high = rounded(moved), rounded(mass)
        pull_ref[:, at] = jnp.concatenate(
            [moved_high, moved - moved_high, mass_high, mass - mass_high], axis=0
        ).astype(bf16)


def near_distances(operand, start, width):
    left_ref, right_ref = operand[:2]
    left = left_ref[start : start + width, :]
    return [jnp.dot(left, right_ref[half], preferred_element_type=f32) for half in range(2)]


def near_pulls(operand, start, width, dist, total):
    pull = operand[2][:, start : start + width]
    weight = [lax.rsqrt((d * d * d).astype(bf16)) for d in dist]
    for half in range(2):
        part = jnp.dot(pull, weight[half], preferred_element_type=f32)
        total[half] = part if total[half] is None else total[half] + part


def near_result(target, total):
    row = row_iota()
    last = row % 4 == 3
    front = row < 4

    def fold(start):
        parts = [t[start : start + 8, :] + t[start + 8 : start + 16, :] for t in total]
        sides = []
        for side in range(2):
            at = slice(side * LANES, (side + 1) * LANES)
            mixed = jnp.where(front, parts[0][:, at], parts[1][:, at])
            sides.append(mixed + pltpu.roll(mixed, 4, 0))
        return jnp.where(front, sides[0], sides[1])

    return jnp.where(last, 0.0, fold(0) - target * fold(16))


def near_kernel(second, sub_count, bucket_count, near_count, me_ref, work_ref, list_ref, *refs):
    refs = list(refs)
    table_refs = [refs.pop(0) for _ in range(sub_count)]
    if second:
        mass_refs = [refs.pop(0) for _ in range(sub_count)]
        acc_refs = [refs.pop(0) for _ in range(sub_count)]
    out_ref, tile_ref = refs[:2]
    refs = refs[2:]
    group_ref, sem = refs[:2]
    operands = [refs[2 + 4 * k : 6 + 4 * k] for k in range(4)]
    me = me_ref[0]
    copies = [
        pltpu.make_async_copy(
            table_refs[k], group_ref.at[pl.ds(k * bucket_count, bucket_count)], sem.at[k]
        )
        for k in range(sub_count)
    ]
    if second:
        base_ref = refs[2 + 4 * 4]
        copies += [
            pltpu.make_async_copy(
                mass_refs[k],
                base_ref.at[pl.ds(k * bucket_count, bucket_count)],
                sem.at[sub_count + k],
            )
            for k in range(sub_count)
        ]
    for copy in copies:
        copy.start()
    for copy in copies:
        copy.wait()
    if second:
        last = row_iota() % 4 == 3
        for part in range(sub_count):

            @pl.loop(0, work_ref.shape[1], unroll=4)
            def _(i):
                slot = other_slot(work_ref[part, i], bucket_count, me)
                tile = group_ref[slot]
                act = jnp.where(last, tile, 0.0)
                act = act + pltpu.roll(act, 7, 0) + pltpu.roll(act, 6, 0) + pltpu.roll(act, 5, 0)
                group_ref[slot] = tile + (DT * DT) * act * acc_refs[part][i]

        @pl.loop(0, sub_count * bucket_count // 8, unroll=2)
        def _(i):
            at = pl.ds(i * 8, 8)
            wide = lax.broadcasted_iota(jnp.int32, (8, 8, LANES), 1) % 4 == 3
            group_ref[at] = jnp.where(wide, base_ref[at], group_ref[at])

    def prepare(i, slot):
        tile = group_ref[other_slot(work_ref[0, i], bucket_count, me)]
        tile_ref[i] = tile
        prepare_near(tile, [group_ref[list_ref[i, k]] for k in range(near_count)], *operands[slot])

    count = work_ref.shape[1]
    span = 4
    width = 2 * LANES
    rows = near_count * LANES
    prepare(0, 0)

    @pl.loop(0, pl.cdiv(count, span))
    def _(block):
        steps = [(part, start) for part in range(span) for start in range(0, rows, width)]
        first = block * span
        totals = {}

        def finish(part, start, dist):
            near_pulls(operands[part], start, width, dist, totals[part])
            if start + width == rows:
                target = operands[part][3][...]
                out_ref[jnp.minimum(first + part, count - 1)] = near_result(target, totals[part])

        pending = None
        for part, start in steps:
            if start == 0:
                totals[part] = [None, None]
            if start == width and part + 1 < span:
                prepare(jnp.minimum(first + part + 1, count - 1), part + 1)
            dist = near_distances(operands[part], start, width)
            if pending is not None:
                finish(*pending)
            pending = (part, start, dist)
        prepare(jnp.minimum(first + span, count - 1), 0)
        finish(*pending)


def splat_operand():
    shape = (PARTS, 7 * LANES)
    row = lax.broadcasted_iota(jnp.int32, shape, 0)
    number = lax.broadcasted_iota(jnp.int32, shape, 1) // LANES
    wanted = jnp.where(number == 0, 0, number + 3)
    keep = jnp.logical_and(row % ROWS == wanted, row < 3 * ROWS)
    return jnp.where(keep, 1.0, 0.0).astype(bf16)


def centre_operand():
    shape = (3 * ROWS, 6 * LANES)
    row = lax.broadcasted_iota(jnp.int32, shape, 0)
    number = lax.broadcasted_iota(jnp.int32, shape, 1) // (2 * LANES)
    return jnp.where(row % ROWS == number + 1, -1.0, 0.0).astype(bf16)


def cells_kernel(
    build,
    near_count,
    cell_count,
    top_count,
    list_ref,
    ess_ref,
    cells_ref,
    tile_ref,
    near_ref,
    out_ref,
    splat_ref,
    *slots,
):
    rows_ref = cells_ref
    if build:
        rows_ref = slots[4]
        build_rows(cells_ref, *slots[4:])
    splat_ref[...] = splat_operand()
    for side in range(2):
        slots[2 * side + 1][: 3 * ROWS, :] = centre_operand()
    count = tile_ref.shape[0]
    total = cell_count + top_count

    def pick_rows(i, slot, start, stop):
        picked_ref = slots[2 * slot]
        for k in range(start, stop):
            index = list_ref[i, near_count + k]
            if k < cell_count:
                index = ess_ref[index]
            picked_ref[pl.ds(k, 1), :] = rows_ref[pl.ds(index, 1), :]

    def place(i, slot):
        places_ref = slots[2 * slot + 1]
        parts = three(tile_ref[i])
        row = row_iota((ROWS, LANES))
        for half in range(2):
            for a in range(3):
                at = 4 * half + a
                spread = [jnp.broadcast_to(p[at : at + 1, :], (ROWS, LANES)) for p in parts]
                value = jnp.where(
                    row == 0,
                    spread[0],
                    jnp.where(row == 1, spread[1], jnp.where(row == 2, spread[2], 0.0)),
                )
                lanes = slice((2 * a + half) * LANES, (2 * a + half + 1) * LANES)
                places_ref[3 * ROWS :, lanes] = value.astype(bf16)

    def spread_cells(slot, start):
        picked_ref, places_ref = slots[2 * slot : 2 * slot + 2]
        left = picked_ref[start : start + CELL_CHUNK, :PARTS].astype(bf16)
        return (
            jnp.dot(left, splat_ref[...], preferred_element_type=f32),
            jnp.dot(left, places_ref[...], preferred_element_type=f32),
        )

    def finish(i, sums):
        row = row_iota()
        result = near_ref[i]
        for half in range(2):
            for a in range(3):
                value = jnp.sum(sums[half][a], axis=0, keepdims=True)
                value = jnp.broadcast_to(value, (8, LANES))
                result += jnp.where(row == 4 * half + a, value, 0.0)
        out_ref[i] = result

    pick_rows(0, 0, 0, total)
    place(0, 0)
    chunks = range(0, total, CELL_CHUNK)
    early = (len(chunks) - 1) * CELL_CHUNK // 8
    share = -(-total // early)

    @pl.loop(0, pl.cdiv(count, CELL_SPAN))
    def _(block):
        item = [jnp.minimum(CELL_SPAN * block + k, count - 1) for k in range(CELL_SPAN + 1)]
        waiting = spread_cells(0, 0)
        for step in range(CELL_SPAN):
            slot = step % 2
            sums = [[jnp.zeros((8, LANES), f32) for _ in range(3)] for _ in range(2)]
            done = 0
            place(item[step + 1], 1 - slot)
            for start in chunks:
                splats, offs = waiting
                if start + CELL_CHUNK < total:
                    waiting = spread_cells(slot, start + CELL_CHUNK)
                elif step + 1 < CELL_SPAN:
                    waiting = spread_cells(1 - slot, 0)
                for group in range(CELL_CHUNK // 8):
                    rows = slice(8 * group, 8 * group + 8)
                    number = [splats[rows, q * LANES : (q + 1) * LANES] for q in range(7)]
                    for half in range(2):
                        off = [
                            offs[rows, (2 * a + half) * LANES : (2 * a + half + 1) * LANES]
                            for a in range(3)
                        ]
                        cell_terms(off, number[0], number[1:], sums[half])
                    if done < total:
                        pick_rows(item[step + 1], 1 - slot, done, min(done + share, total))
                        done += share
            finish(item[step], sums)


def body(
    positions,
    velocities,
    masses,
    accel_prev,
    active,
    bucket_top,
    near_list,
    cell_list,
    top_list,
    essential,
    work,
):
    bucket_count = bucket_top.shape[0]
    sub_count = lax.axis_size("sub")
    dom_count = lax.axis_size("dom")
    me = lax.axis_index("sub").astype(jnp.int32)
    group_buckets = sub_count * bucket_count
    device_count = sub_count * dom_count
    near_count, cell_count, top_count = near_list.shape[1], cell_list.shape[1], top_list.shape[1]
    work_count = work.shape[0]
    vmem = pl.BlockSpec(memory_space=pltpu.VMEM)
    smem = pl.BlockSpec(memory_space=pltpu.SMEM)
    anywhere = pl.BlockSpec(memory_space=pl.ANY)
    work_shape = jax.ShapeDtypeStruct((work_count, 8, LANES), f32)
    sent_shape = jax.ShapeDtypeStruct((device_count * bucket_count // LANES * SENT, LANES), f32)

    activity = active.astype(f32)
    half_speed = velocities + 0.5 * DT * activity * accel_prev
    places = positions + DT * half_speed
    tiles = to_tiles(places, masses)
    ahead = to_tiles(places + DT * half_speed, activity)
    speeds = to_tiles(half_speed, activity)

    near_list, cell_list, top_list, essential, work, _ = lax.optimization_barrier(
        (near_list, cell_list, top_list, essential, work, tiles)
    )
    lists = jnp.concatenate([near_list, cell_list, top_list], axis=1)
    lists = jnp.pad(lists, ((0, 0), (0, -lists.shape[1] % LANES)))
    wanted = essential.reshape(dom_count, -1) + (
        jnp.arange(dom_count, dtype=jnp.int32) * group_buckets
    )[:, None]
    wanted = wanted.reshape(-1)
    extra = jnp.concatenate([wanted, work])
    extra = jnp.pad(extra, (0, -extra.shape[0] % LANES))
    sent = jnp.concatenate([lists.reshape(-1), extra])
    tops_row = bucket_top.astype(f32)[None]

    table = sub_gather(tiles, sub_count)
    own = pl.pallas_call(
        first_moments_kernel,
        out_shape=sent_shape,
        in_specs=[vmem] * 2,
        out_specs=vmem,
        name="first_moments",
    )(tiles.reshape(-1, LANES), tops_row)

    def exchange(rows):
        wide = rows.reshape(device_count, -1)
        got = lax.all_to_all(wide, ("dom", "sub"), split_axis=0, concat_axis=0, tiled=True)
        return got.reshape(-1, LANES)

    cells = exchange(own)
    list_parts = sub_gather(sent, sub_count)
    ahead_sent, _ = lax.optimization_barrier((ahead, cells))
    table_ahead = sub_gather(ahead_sent, sub_count)

    width = lists.shape[1]
    list_table = jnp.stack(
        [part[: bucket_count * width].reshape(bucket_count, width) for part in list_parts]
    ).reshape(group_buckets, width)
    ess_all = jnp.concatenate(
        [part[bucket_count * width :][: wanted.shape[0]] for part in list_parts]
    )
    work_all = jnp.stack(
        [part[bucket_count * width + wanted.shape[0] :][:work_count] for part in list_parts]
    )
    work_lists = jnp.take(list_table, other_slot(work, bucket_count, me), axis=0)
    column = jnp.arange(width)[None]
    work_lists = jnp.where(
        column < near_count,
        other_slot(work_lists, bucket_count, me),
        jnp.where(
            column < near_count + cell_count,
            other_slot(work_lists, wanted.shape[0], me),
            work_lists + device_count * bucket_count,
        ),
    )
    me_one = me[None]

    def near_call(second, tables, extra_tables):
        operand = [
            pltpu.VMEM((near_count * LANES, 48), bf16),
            pltpu.VMEM((2, 48, 2 * LANES), bf16),
            pltpu.VMEM((32, near_count * LANES), bf16),
            pltpu.VMEM((8, LANES), f32),
        ]
        scratch = [
            pltpu.VMEM((group_buckets, 8, LANES), f32),
            pltpu.SemaphoreType.DMA((2 * sub_count,)),
        ] + operand * 4
        specs = [smem] * 3 + [anywhere] * sub_count
        if second:
            specs += [anywhere] * sub_count + [vmem] * sub_count
            scratch.append(pltpu.VMEM((group_buckets, 8, LANES), f32))
        return pl.pallas_call(
            functools.partial(near_kernel, second, sub_count, bucket_count, near_count),
            out_shape=(work_shape, work_shape),
            in_specs=specs,
            out_specs=(vmem, vmem),
            scratch_shapes=scratch,
            name="near_second" if second else "near_first",
        )(me_one, work_all, work_lists, *tables, *extra_tables)

    def table_scratch(buckets):
        return [
            pltpu.VMEM((ROWS * buckets // LANES, LANES), f32),
            pltpu.VMEM((TOP // LOWER * ROWS, LOWER), f32),
            pltpu.VMEM((TOP // LOWER * ROWS, LOWER), f32),
        ]

    def table_call(cells):
        buckets = cells.shape[0] // SENT * LANES
        return pl.pallas_call(
            build_rows,
            out_shape=jax.ShapeDtypeStruct((buckets + TOP, LANES), f32),
            in_specs=[vmem],
            out_specs=vmem,
            scratch_shapes=table_scratch(buckets),
            name="cell_table",
        )(cells)

    def cells_call(build, cells, tile, near):
        buckets = cells.shape[0] // SENT * LANES
        scratch = [pltpu.VMEM((PARTS, 7 * LANES), bf16)] + [
            pltpu.VMEM((cell_count + top_count, LANES), f32),
            pltpu.VMEM((PARTS, 6 * LANES), bf16),
        ] * 2
        if build:
            scratch += [pltpu.VMEM((buckets + TOP, LANES), f32), *table_scratch(buckets)]
        return pl.pallas_call(
            functools.partial(cells_kernel, build, near_count, cell_count, top_count),
            out_shape=work_shape,
            in_specs=[smem] * 2 + [vmem] * 3,
            out_specs=vmem,
            scratch_shapes=scratch,
            name="cell_force",
        )(work_lists, ess_all, cells, tile, near)

    cell_table = table_call(cells)
    near, tile = near_call(False, table, [])
    acc_one = sub_gather(cells_call(False, cell_table, tile, near), sub_count)
    flat_shape = jax.ShapeDtypeStruct((bucket_count * 8, LANES), f32)
    own_shape = jax.ShapeDtypeStruct(((bucket_count + 1) * 8, LANES), f32)

    def flat(values):
        return values.reshape(-1, LANES)

    own, places_two, own_one = pl.pallas_call(
        functools.partial(second_moments_kernel, sub_count),
        out_shape=(sent_shape, flat_shape, own_shape),
        in_specs=[smem] * 2 + [vmem] * (3 + sub_count),
        out_specs=(vmem, vmem, vmem),
        name="second_moments",
    )(me_one, work_all, flat(ahead), flat(tiles), tops_row, *acc_one)
    cells = exchange(own)
    near, tile = near_call(True, table_ahead, [*table, *acc_one])
    acc_two = sub_gather(cells_call(True, cells, tile, near), sub_count)
    speed_two = pl.pallas_call(
        functools.partial(final_kernel, sub_count),
        out_shape=flat_shape,
        in_specs=[smem] * 2 + [vmem] * (2 + sub_count),
        out_specs=vmem,
        scratch_shapes=[pltpu.VMEM(own_shape.shape, f32)],
        name="final_speeds",
    )(me_one, work_all, flat(speeds), own_one, *acc_two)
    return (
        from_tiles(speed_two.reshape(-1, 8, LANES)),
        from_tiles(places_two.reshape(-1, 8, LANES)),
    )


def solution(mesh):
    both = ("dom", "sub")
    in_specs = (
        P(None, both),
        P(None, both),
        P(both),
        P(None, both),
        P(both),
        P(both),
        P(both, None),
        P(both, None),
        P(both, None),
        P("dom", "sub", None, None),
        P(both),
    )
    out_specs = (P(None, both), P(None, both))
    return jax.shard_map(body, mesh=mesh, in_specs=in_specs, out_specs=out_specs, check_vma=False)
```

```python
import functools

import jax
import jax.numpy as jnp
from jax import lax
from jax.experimental import pallas as pl
from jax.experimental.pallas import tpu as pltpu
from jax.sharding import PartitionSpec as P


TOP_SIDE = 16
TOP = TOP_SIDE**3
DT = 0.01
EPS = 0.0025
MASS_FLOOR = 0.5
LANES = 128
ROWS = 16
SENT = 11
LOWER = 256
PARTS = 4 * ROWS
CHUNKS = 1
CELL_CHUNK = 32
CELL_SPAN = 4


f32 = jnp.float32
bf16 = jnp.bfloat16


def other_slot(index, size, me):
    if size & (size - 1) == 0:
        return index ^ (me * size)
    return ((index // size) ^ me) * size + index % size


def to_tiles(three, one):
    flat = jnp.concatenate([three, one[None]], axis=0)
    count = flat.shape[1] // (2 * LANES)
    return flat.reshape(4, count, 2, LANES).transpose(1, 2, 0, 3).reshape(count, 8, LANES)


def from_tiles(tiles):
    count = tiles.shape[0]
    flat = tiles.reshape(count, 2, 4, LANES).transpose(2, 0, 1, 3).reshape(4, count * 2 * LANES)
    return flat[:3]


def sub_gather(block, sub_count, before_pass=None):
    parts = [None] * sub_count
    parts[0] = block
    for step in range(0, sub_count, 2):
        if step:
            parts[step] = lax.ppermute(block, "sub", [(i, i ^ step) for i in range(sub_count)])
            if before_pass is not None:
                parts[step], _ = lax.optimization_barrier((parts[step], before_pass))
    for step in range(0, sub_count, 2):
        parts[step + 1] = lax.ppermute(parts[step], "sub", [(i, i ^ 1) for i in range(sub_count)])
    return parts


def row_iota(shape=(8, LANES)):
    return lax.broadcasted_iota(jnp.int32, shape, 0)


def rounded(values):
    return values.astype(bf16).astype(f32)


def moments_of(get):
    weights = [get(0, 3), get(1, 3)]
    places = [[get(half, axis) for axis in range(3)] for half in range(2)]

    def total(one, two):
        return jnp.sum(one + two, axis=1, keepdims=True)

    mass = total(weights[0], weights[1])
    centre = [
        total(weights[0] * places[0][axis], weights[1] * places[1][axis]) / mass
        for axis in range(3)
    ]
    off = [[places[half][axis] - centre[axis] for axis in range(3)] for half in range(2)]
    woff = [[weights[half] * off[half][axis] for axis in range(3)] for half in range(2)]

    def second(a, b):
        return total(woff[0][a] * off[0][b], woff[1][a] * off[1][b])

    xx, yy, zz = second(0, 0), second(1, 1), second(2, 2)
    trace = xx + yy + zz
    return [mass] + centre + [
        3.0 * xx - trace,
        3.0 * yy - trace,
        3.0 * zz - trace,
        3.0 * second(0, 1),
        3.0 * second(0, 2),
        3.0 * second(1, 2),
    ]


def write_moments(columns, tops_row, out_ref, bucket_count):
    lane = lax.broadcasted_iota(jnp.int32, (bucket_count, LANES), 1)
    wide = jnp.zeros((bucket_count, LANES), f32)
    for q, column in enumerate(columns):
        wide = jnp.where(lane == q, column, wide)
    turned = jnp.transpose(wide)
    blocks = bucket_count // LANES
    for block in range(blocks):
        at = slice(block * LANES, (block + 1) * LANES)
        rows = jnp.concatenate([turned[:10, at], tops_row[:, at]], axis=0)
        for copy in range(out_ref.shape[0] // (blocks * SENT)):
            start = (copy * blocks + block) * SENT
            out_ref[start : start + SENT, :] = rows


def tile_rows(ref, row, bucket_count):
    return ref[pl.ds(row, bucket_count, stride=8), :]


def first_moments_kernel(tiles_ref, tops_ref, out_ref):
    bucket_count = tiles_ref.shape[0] // 8
    columns = moments_of(lambda half, row: tile_rows(tiles_ref, 4 * half + row, bucket_count))
    write_moments(columns, tops_ref[...], out_ref, bucket_count)


def spread_own(acc_refs, work_ref, me, own_ref, bucket_count):
    own_ref[...] = jnp.zeros_like(own_ref)
    count = work_ref.shape[1]
    for part, acc_ref in enumerate(acc_refs):

        @pl.loop(0, count, unroll=8 if count % 8 == 0 else 1)
        def _(i):
            bucket = work_ref[part, i] - me * bucket_count
            mine = jnp.logical_and(bucket >= 0, bucket < bucket_count)
            slot = pl.multiple_of(jnp.where(mine, bucket, bucket_count) * 8, 8)
            own_ref[pl.ds(slot, 8), :] = acc_ref[i]


def act_rows(tiles):
    count = tiles.shape[0] // 8
    wide = tiles.reshape(count, 8, LANES)
    row = lax.broadcasted_iota(jnp.int32, wide.shape, 1)
    first = jnp.broadcast_to(wide[:, 3:4, :], wide.shape)
    second = jnp.broadcast_to(wide[:, 7:8, :], wide.shape)
    return row % 4 == 3, jnp.where(row < 4, first, second), wide


def second_moments_kernel(
    sub_count, me_ref, work_ref, ahead_ref, tiles_ref, speeds_ref, tops_ref, *refs
):
    acc_refs, (out_ref, places_ref, base_ref, own_ref) = refs[:sub_count], refs[sub_count:]
    bucket_count = tiles_ref.shape[0] // 8
    spread_own(acc_refs, work_ref, me_ref[0], own_ref, bucket_count)

    @pl.loop(0, bucket_count // 8)
    def _(i):
        at = pl.ds(pl.multiple_of(i * 64, 64), 64)
        last, act, ahead = act_rows(ahead_ref[at, :])
        kick = DT * act * own_ref[at, :].reshape(8, 8, LANES)
        base_ref[at, :] = speeds_ref[at, :] + jnp.where(last, 0.0, kick).reshape(64, LANES)
        moved = ahead + DT * kick
        places = jnp.where(last, tiles_ref[at, :].reshape(8, 8, LANES), moved)
        places_ref[at, :] = places.reshape(64, LANES)

    columns = moments_of(lambda half, row: tile_rows(places_ref, 4 * half + row, bucket_count))
    write_moments(columns, tops_ref[...], out_ref, bucket_count)


def final_kernel(sub_count, me_ref, work_ref, base_ref, *refs):
    acc_refs, (out_ref, full_ref) = refs[:sub_count], refs[sub_count:]
    bucket_count = base_ref.shape[0] // 8
    full_ref[: bucket_count * 8, :] = base_ref[...]
    count = work_ref.shape[1]
    last = row_iota() % 4 == 3
    for part, acc_ref in enumerate(acc_refs):

        @pl.loop(0, count, unroll=8 if count % 8 == 0 else 1)
        def _(i):
            bucket = work_ref[part, i] - me_ref[0] * bucket_count
            mine = jnp.logical_and(bucket >= 0, bucket < bucket_count)
            tile = base_ref[pl.ds(pl.multiple_of(jnp.where(mine, bucket, 0) * 8, 8), 8), :]
            act = jnp.where(last, tile, 0.0)
            act = act + pltpu.roll(act, 7, 0) + pltpu.roll(act, 6, 0) + pltpu.roll(act, 5, 0)
            place = pl.ds(pl.multiple_of(jnp.where(mine, bucket, bucket_count) * 8, 8), 8)
            full_ref[place, :] = tile + (0.5 * DT) * act * acc_ref[i]

    out_ref[...] = full_ref[: bucket_count * 8, :]


def traceless(diag, cross):
    trace = diag[0] + diag[1] + diag[2]
    return [3.0 * d - trace for d in diag] + [3.0 * c for c in cross]


def outer(first, second):
    return (
        [first[a] * second[a] for a in range(3)],
        [first[0] * second[1], first[0] * second[2], first[1] * second[2]],
    )


def in_parts(values):
    high, middle, low = three(values)
    return jnp.concatenate([high, middle, low, jnp.ones_like(values)], axis=0)


def build_rows(cells_ref, rows_ref, raw_ref, sums_ref, tops_ref):
    blocks = cells_ref.shape[0] // SENT
    uppers = TOP // LOWER
    sides = LOWER // LANES
    for block in range(blocks):
        start = block * SENT
        if start + ROWS <= cells_ref.shape[0]:
            turned = cells_ref[start : start + ROWS, :]
        else:
            turned = jnp.concatenate(
                [cells_ref[start : start + SENT, :], jnp.zeros((ROWS - SENT, LANES), f32)], axis=0
            )
        rows_ref[block * LANES : (block + 1) * LANES, :PARTS] = jnp.transpose(in_parts(turned))
    side = TOP_SIDE

    def sent(q):
        return cells_ref[pl.ds(q, blocks, stride=SENT), :]

    top_id = sent(10).astype(jnp.int32)
    index = [top_id // (side * side), top_id // side % side, top_id % side]
    mass = sent(0)
    delta = [sent(1 + a) - (index[a].astype(f32) + 0.5) / side for a in range(3)]
    first = [mass * delta[a] for a in range(3)]
    lifted = traceless(*outer(first, delta))
    raw = [mass] + first + [sent(4 + k) + lifted[k] for k in range(6)]
    for q in range(ROWS):
        raw_ref[q * blocks : (q + 1) * blocks, :] = raw[q] if q < 10 else jnp.zeros_like(mass)
    sums_ref[...] = jnp.zeros_like(sums_ref)
    pair = 2 if blocks % 2 == 0 else 1

    @pl.loop(0, blocks // pair)
    def _(step):
        top, values = [], []
        for part in range(pair):
            block = step * pair + part
            top.append(cells_ref[pl.ds(block * SENT + 10, 1), :])
            values.append(raw_ref[pl.ds(block, ROWS, stride=blocks), :])
        top = jnp.concatenate(top, axis=1).astype(jnp.int32)
        values = jnp.concatenate(values, axis=1)
        high = values.astype(bf16)
        low = (values - high.astype(f32)).astype(bf16)
        width = top.shape[1]
        upper = jnp.broadcast_to(top // LOWER, (ROWS, width))
        lower = jnp.broadcast_to(top % LOWER, (LOWER, width))
        match = lax.broadcasted_iota(jnp.int32, (LOWER, width), 0) == lower
        picks = jnp.where(match, 1.0, 0.0).astype(bf16)
        empty = jnp.zeros_like(high)
        parts = []
        for piece in (high, low):
            left = jnp.concatenate(
                [jnp.where(upper == u, piece, empty) for u in range(uppers)], axis=0
            )
            parts.append(
                lax.dot_general(left, picks, (((1,), (1,)), ((), ())), preferred_element_type=f32)
            )
        both = parts[0] + parts[1]
        for side_at in range(sides):
            rows = slice(side_at * uppers * ROWS, (side_at + 1) * uppers * ROWS)
            sums_ref[rows, :] += both[:, side_at * LANES : (side_at + 1) * LANES]

    cell = lax.broadcasted_iota(jnp.int32, (uppers, LOWER), 0) * LOWER
    cell = cell + lax.broadcasted_iota(jnp.int32, (uppers, LOWER), 1)
    index = [cell // (side * side), cell // side % side, cell % side]

    def summed(q):
        return jnp.concatenate(
            [
                sums_ref[pl.ds(side_at * uppers * ROWS + q, uppers, stride=ROWS), :]
                for side_at in range(sides)
            ],
            axis=1,
        )

    mass = summed(0)
    inverse = 1.0 / jnp.maximum(mass, MASS_FLOOR)
    first = [summed(1 + a) for a in range(3)]
    shift = [first[a] * inverse for a in range(3)]
    lowered = traceless(*outer(first, shift))
    tops = (
        [mass]
        + [(index[a].astype(f32) + 0.5) / side + shift[a] for a in range(3)]
        + [summed(4 + k) - lowered[k] for k in range(6)]
    )
    for q in range(10):
        for side_at in range(sides):
            at = pl.ds(side_at * uppers * ROWS + q, uppers, stride=ROWS)
            tops_ref[at, :] = tops[q][:, side_at * LANES : (side_at + 1) * LANES]
    for u in range(uppers):
        for side_at in range(sides):
            start = blocks * LANES + u * LOWER + side_at * LANES
            rows = (side_at * uppers + u) * ROWS
            rows_ref[start : start + LANES, :PARTS] = jnp.transpose(
                in_parts(tops_ref[rows : rows + ROWS, :])
            )


def cell_terms(off, mass, quad, sums):
    dist = off[0] * off[0] + off[1] * off[1] + off[2] * off[2] + EPS
    inv = lax.rsqrt(dist)
    inv_two = inv * inv
    inv_five = inv_two * inv_two * inv
    along = [
        quad[0] * off[0] + quad[3] * off[1] + quad[4] * off[2],
        quad[3] * off[0] + quad[1] * off[1] + quad[5] * off[2],
        quad[4] * off[0] + quad[5] * off[1] + quad[2] * off[2],
    ]
    both = off[0] * along[0] + off[1] * along[1] + off[2] * along[2]
    radial = mass * dist + 2.5 * both * inv_two
    for a in range(3):
        sums[a] += (along[a] - radial * off[a]) * inv_five


def with_norm(values, extra, scale, last):
    squares = jnp.where(last, 0.0, values * values)
    norm = pltpu.roll(squares, 1, 0) + pltpu.roll(squares, 2, 0) + pltpu.roll(squares, 3, 0)
    return jnp.where(last, norm + extra, scale * values)


def three(values):
    high = rounded(values)
    rest = values - high
    middle = rounded(rest)
    return high, middle, rest - middle


def prepare_near(tile, sources, masses, left_ref, right_ref, pull_ref, target_ref):
    row = row_iota()
    last = row % 4 == 3
    front = row < 4
    mean = jnp.sum(tile, axis=1, keepdims=True)
    mean = jnp.broadcast_to(mean, (8, LANES))
    centre = jnp.where(last, 0.0, (mean + pltpu.roll(mean, 4, 0)) * (0.5 / LANES))
    target = tile - centre
    target_ref[...] = target
    high, middle, low = three(with_norm(target, EPS, -2.0, last))
    plain = jnp.where(last, 1.0, high)
    blocks = [plain, plain, plain, jnp.where(last, high, middle), middle, low]
    turned = [pltpu.roll(block, 4, 0) for block in blocks]
    first = [jnp.where(front, b, t) for b, t in zip(blocks, turned)]
    second = [jnp.where(front, t, b) for b, t in zip(blocks, turned)]
    for half in range(2):
        keep = front if half == 0 else jnp.logical_not(front)
        for side, parts in enumerate((first, second)):
            right_ref[half, :, side * LANES : (side + 1) * LANES] = jnp.concatenate(
                [jnp.where(keep, part, 0.0) for part in parts], axis=0
            ).astype(bf16)
    for k, (source, weights) in enumerate(zip(sources, masses)):
        at = slice(k * LANES, (k + 1) * LANES)
        place = source - centre
        high, middle, low = three(with_norm(place, 0.0, 1.0, last))
        high_one = jnp.where(last, 1.0, high)
        middle_one = jnp.where(last, 1.0, middle)
        stack = jnp.concatenate([high, middle, low, high_one, middle_one, high_one], axis=0)
        left_ref[at, :] = jnp.transpose(stack).astype(bf16)
        mass = jnp.where(last, weights, 0.0)
        mass = mass + pltpu.roll(mass, 7, 0) + pltpu.roll(mass, 6, 0) + pltpu.roll(mass, 5, 0)
        moved = mass * place
        moved_high, mass_high = rounded(moved), rounded(mass)
        pull_ref[:, at] = jnp.concatenate(
            [moved_high, moved - moved_high, mass_high, mass - mass_high], axis=0
        ).astype(bf16)


def near_distances(operand, start, width):
    left_ref, right_ref = operand[:2]
    left = left_ref[start : start + width, :]
    return [jnp.dot(left, right_ref[half], preferred_element_type=f32) for half in range(2)]


def near_pulls(operand, start, width, dist, total):
    pull = operand[2][:, start : start + width]
    weight = [lax.rsqrt((d * d * d).astype(bf16)) for d in dist]
    for half in range(2):
        part = jnp.dot(pull, weight[half], preferred_element_type=f32)
        total[half] = part if total[half] is None else total[half] + part


def near_result(target, total):
    row = row_iota()
    last = row % 4 == 3
    front = row < 4

    def fold(start):
        parts = [t[start : start + 8, :] + t[start + 8 : start + 16, :] for t in total]
        sides = []
        for side in range(2):
            at = slice(side * LANES, (side + 1) * LANES)
            mixed = jnp.where(front, parts[0][:, at], parts[1][:, at])
            sides.append(mixed + pltpu.roll(mixed, 4, 0))
        return jnp.where(front, sides[0], sides[1])

    return jnp.where(last, 0.0, fold(0) - target * fold(16))


def near_kernel(second, sub_count, bucket_count, near_count, me_ref, work_ref, list_ref, *refs):
    refs = list(refs)
    tables = [refs.pop(0) for _ in range(sub_count * CHUNKS)]
    if second:
        table_refs = [refs.pop(0) for _ in range(sub_count)]
        acc_refs = [refs.pop(0) for _ in range(sub_count)]
    out_ref, tile_ref = refs[:2]
    refs = refs[2:]
    group_ref, sem = refs[:2]
    operands = [refs[2 + 4 * k : 6 + 4 * k] for k in range(4)]
    me = me_ref[0]
    mass_ref = group_ref
    if second:
        mass_ref, acc_ref = refs[2 + 4 * 4 :]
    piece = bucket_count // CHUNKS
    copies = [
        pltpu.make_async_copy(ref, mass_ref.at[pl.ds(k * piece, piece)], sem.at[k])
        for k, ref in enumerate(tables)
    ]
    if second:
        copies += [
            pltpu.make_async_copy(
                table_refs[k],
                group_ref.at[pl.ds(k * bucket_count, bucket_count)],
                sem.at[len(tables) + k],
            )
            for k in range(sub_count)
        ]
        copies += [
            pltpu.make_async_copy(acc_refs[k], acc_ref.at[k], sem.at[len(tables) + sub_count + k])
            for k in range(sub_count)
        ]
    for copy in copies:
        copy.start()
    for copy in copies:
        copy.wait()
    if second:
        last = row_iota() % 4 == 3
        for part in range(sub_count):

            @pl.loop(0, work_ref.shape[1], unroll=4)
            def _(i):
                slot = other_slot(work_ref[part, i], bucket_count, me)
                tile = group_ref[slot]
                act = jnp.where(last, tile, 0.0)
                act = act + pltpu.roll(act, 7, 0) + pltpu.roll(act, 6, 0) + pltpu.roll(act, 5, 0)
                group_ref[slot] = tile + (DT * DT) * act * acc_ref[part, i]

    def prepare(i, slot):
        tile = group_ref[other_slot(work_ref[0, i], bucket_count, me)]
        tile_ref[i] = tile
        slots = [list_ref[i, k] for k in range(near_count)]
        prepare_near(
            tile, [group_ref[n] for n in slots], [mass_ref[n] for n in slots], *operands[slot]
        )

    count = work_ref.shape[1]
    span = 4
    width = 2 * LANES
    rows = near_count * LANES
    prepare(0, 0)

    @pl.loop(0, pl.cdiv(count, span))
    def _(block):
        steps = [(part, start) for part in range(span) for start in range(0, rows, width)]
        first = block * span
        totals = {}

        def finish(part, start, dist):
            near_pulls(operands[part], start, width, dist, totals[part])
            if start + width == rows:
                target = operands[part][3][...]
                out_ref[jnp.minimum(first + part, count - 1)] = near_result(target, totals[part])

        pending = None
        for part, start in steps:
            if start == 0:
                totals[part] = [None, None]
            if start == width and part + 1 < span:
                prepare(jnp.minimum(first + part + 1, count - 1), part + 1)
            dist = near_distances(operands[part], start, width)
            if pending is not None:
                finish(*pending)
            pending = (part, start, dist)
        prepare(jnp.minimum(first + span, count - 1), 0)
        finish(*pending)


def splat_operand():
    shape = (PARTS, 7 * LANES)
    row = lax.broadcasted_iota(jnp.int32, shape, 0)
    number = lax.broadcasted_iota(jnp.int32, shape, 1) // LANES
    wanted = jnp.where(number == 0, 0, number + 3)
    keep = jnp.logical_and(row % ROWS == wanted, row < 3 * ROWS)
    return jnp.where(keep, 1.0, 0.0).astype(bf16)


def centre_operand():
    shape = (3 * ROWS, 6 * LANES)
    row = lax.broadcasted_iota(jnp.int32, shape, 0)
    number = lax.broadcasted_iota(jnp.int32, shape, 1) // (2 * LANES)
    return jnp.where(row % ROWS == number + 1, -1.0, 0.0).astype(bf16)


def cells_kernel(
    near_count,
    cell_count,
    top_count,
    list_ref,
    ess_ref,
    cells_ref,
    tile_ref,
    near_ref,
    out_ref,
    splat_ref,
    *slots,
):
    rows_ref = slots[4]
    build_rows(cells_ref, *slots[4:])
    splat_ref[...] = splat_operand()
    for side in range(2):
        slots[2 * side + 1][: 3 * ROWS, :] = centre_operand()
    count = tile_ref.shape[0]
    total = cell_count + top_count

    def pick_rows(i, slot, start, stop):
        picked_ref = slots[2 * slot]
        for k in range(start, stop):
            index = list_ref[i, near_count + k]
            if k < cell_count:
                index = ess_ref[index]
            picked_ref[pl.ds(k, 1), :] = rows_ref[pl.ds(index, 1), :]

    def place(i, slot):
        places_ref = slots[2 * slot + 1]
        parts = three(tile_ref[i])
        row = row_iota((ROWS, LANES))
        for half in range(2):
            for a in range(3):
                at = 4 * half + a
                spread = [jnp.broadcast_to(p[at : at + 1, :], (ROWS, LANES)) for p in parts]
                value = jnp.where(
                    row == 0,
                    spread[0],
                    jnp.where(row == 1, spread[1], jnp.where(row == 2, spread[2], 0.0)),
                )
                lanes = slice((2 * a + half) * LANES, (2 * a + half + 1) * LANES)
                places_ref[3 * ROWS :, lanes] = value.astype(bf16)

    def spread_cells(slot, start):
        picked_ref, places_ref = slots[2 * slot : 2 * slot + 2]
        left = picked_ref[start : start + CELL_CHUNK, :PARTS].astype(bf16)
        return (
            jnp.dot(left, splat_ref[...], preferred_element_type=f32),
            jnp.dot(left, places_ref[...], preferred_element_type=f32),
        )

    def finish(i, sums):
        row = row_iota()
        result = near_ref[i]
        for half in range(2):
            for a in range(3):
                value = jnp.sum(sums[half][a], axis=0, keepdims=True)
                value = jnp.broadcast_to(value, (8, LANES))
                result += jnp.where(row == 4 * half + a, value, 0.0)
        out_ref[i] = result

    pick_rows(0, 0, 0, total)
    place(0, 0)
    chunks = range(0, total, CELL_CHUNK)
    early = (len(chunks) - 1) * CELL_CHUNK // 8
    share = -(-total // early)

    @pl.loop(0, pl.cdiv(count, CELL_SPAN))
    def _(block):
        item = [jnp.minimum(CELL_SPAN * block + k, count - 1) for k in range(CELL_SPAN + 1)]
        waiting = spread_cells(0, 0)
        for step in range(CELL_SPAN):
            slot = step % 2
            sums = [[jnp.zeros((8, LANES), f32) for _ in range(3)] for _ in range(2)]
            done = 0
            place(item[step + 1], 1 - slot)
            for start in chunks:
                splats, offs = waiting
                if start + CELL_CHUNK < total:
                    waiting = spread_cells(slot, start + CELL_CHUNK)
                elif step + 1 < CELL_SPAN:
                    waiting = spread_cells(1 - slot, 0)
                for group in range(CELL_CHUNK // 8):
                    rows = slice(8 * group, 8 * group + 8)
                    number = [splats[rows, q * LANES : (q + 1) * LANES] for q in range(7)]
                    for half in range(2):
                        off = [
                            offs[rows, (2 * a + half) * LANES : (2 * a + half + 1) * LANES]
                            for a in range(3)
                        ]
                        cell_terms(off, number[0], number[1:], sums[half])
                    if done < total:
                        pick_rows(item[step + 1], 1 - slot, done, min(done + share, total))
                        done += share
            finish(item[step], sums)


def body(
    positions,
    velocities,
    masses,
    accel_prev,
    active,
    bucket_top,
    near_list,
    cell_list,
    top_list,
    essential,
    work,
):
    bucket_count = bucket_top.shape[0]
    sub_count = lax.axis_size("sub")
    dom_count = lax.axis_size("dom")
    me = lax.axis_index("sub").astype(jnp.int32)
    group_buckets = sub_count * bucket_count
    device_count = sub_count * dom_count
    near_count, cell_count, top_count = near_list.shape[1], cell_list.shape[1], top_list.shape[1]
    work_count = work.shape[0]
    vmem = pl.BlockSpec(memory_space=pltpu.VMEM)
    smem = pl.BlockSpec(memory_space=pltpu.SMEM)
    anywhere = pl.BlockSpec(memory_space=pl.ANY)
    work_shape = jax.ShapeDtypeStruct((work_count, 8, LANES), f32)
    sent_shape = jax.ShapeDtypeStruct((device_count * bucket_count // LANES * SENT, LANES), f32)

    activity = active.astype(f32)
    half_speed = velocities + 0.5 * DT * activity * accel_prev
    places = positions + DT * half_speed
    tiles = to_tiles(places, masses)
    places, half_speed, activity, _ = lax.optimization_barrier(
        (places, half_speed, activity, tiles)
    )
    ahead = to_tiles(places + DT * half_speed, activity)
    speeds = to_tiles(half_speed, activity)

    tops_row = bucket_top.astype(f32)[None]

    own = pl.pallas_call(
        first_moments_kernel,
        out_shape=sent_shape,
        in_specs=[vmem] * 2,
        out_specs=vmem,
        name="first_moments",
    )(tiles.reshape(-1, LANES), tops_row)

    def exchange(rows):
        wide = rows.reshape(device_count, -1)
        got = lax.all_to_all(wide, ("dom", "sub"), split_axis=0, concat_axis=0, tiled=True)
        return got.reshape(-1, LANES)

    cells = exchange(own)
    near_list, cell_list, top_list, essential, work, _ = lax.optimization_barrier(
        (near_list, cell_list, top_list, essential, work, own)
    )

    def as_rows(values):
        return jnp.pad(values, (0, -values.shape[0] % LANES)).reshape(-1, LANES)

    lists = jnp.concatenate([near_list, cell_list, top_list], axis=1)
    lists = jnp.pad(lists, ((0, 0), (0, -lists.shape[1] % LANES)))
    width = lists.shape[1]
    wanted = essential.reshape(dom_count, -1) + (
        jnp.arange(dom_count, dtype=jnp.int32) * group_buckets
    )[:, None]
    ess_size = wanted.size
    list_rows = bucket_count * width // LANES
    ess_rows = -(-ess_size // LANES)
    sent = jnp.concatenate(
        [lists.reshape(-1, LANES), as_rows(wanted.reshape(-1)), as_rows(work)], axis=0
    )
    sent_rows = sent.shape[0]
    sent = jnp.pad(sent, ((0, -sent_rows % 8), (0, 0)))
    all_rows = jnp.stack(sub_gather(sent, sub_count))
    ess_all = all_rows[:, list_rows : list_rows + ess_rows].reshape(sub_count, -1)
    ess_all = ess_all[:, :ess_size].reshape(-1)
    work_all = all_rows[:, list_rows + ess_rows : sent_rows].reshape(sub_count, -1)
    work_all = work_all[:, :work_count]
    mine = other_slot(work, bucket_count, me)
    if width == LANES:
        index = mine // bucket_count * sent.shape[0] + mine % bucket_count
        work_lists = jnp.take(all_rows.reshape(-1, LANES), index, axis=0)
    else:
        list_table = all_rows[:, :list_rows].reshape(group_buckets, width)
        work_lists = jnp.take(list_table, mine, axis=0)
    column = jnp.arange(width)[None]
    work_lists = jnp.where(
        column < near_count,
        other_slot(work_lists, bucket_count, me),
        jnp.where(
            column < near_count + cell_count,
            other_slot(work_lists, ess_size, me),
            work_lists + device_count * bucket_count,
        ),
    )
    piece = bucket_count // CHUNKS
    pieces = [sub_gather(tiles[c * piece : (c + 1) * piece], sub_count, work_lists) for c in range(CHUNKS)]
    table = [pieces[c][k] for k in range(sub_count) for c in range(CHUNKS)]
    ahead_sent, _ = lax.optimization_barrier((ahead, table))
    table_ahead = sub_gather(ahead_sent, sub_count)

    me_one = me[None]

    def near_call(second, extra_tables):
        operand = [
            pltpu.VMEM((near_count * LANES, 48), bf16),
            pltpu.VMEM((2, 48, 2 * LANES), bf16),
            pltpu.VMEM((32, near_count * LANES), bf16),
            pltpu.VMEM((8, LANES), f32),
        ]
        scratch = [
            pltpu.VMEM((group_buckets, 8, LANES), f32),
            pltpu.SemaphoreType.DMA(((2 + CHUNKS) * sub_count,)),
        ] + operand * 4
        specs = [smem] * 3 + [anywhere] * (sub_count * CHUNKS)
        if second:
            specs += [anywhere] * (2 * sub_count)
            scratch += [
                pltpu.VMEM((group_buckets, 8, LANES), f32),
                pltpu.VMEM((sub_count, work_count, 8, LANES), f32),
            ]
        return pl.pallas_call(
            functools.partial(near_kernel, second, sub_count, bucket_count, near_count),
            out_shape=(work_shape, work_shape),
            in_specs=specs,
            out_specs=(vmem, vmem),
            scratch_shapes=scratch,
            name="near_second" if second else "near_first",
        )(me_one, work_all, work_lists, *table, *extra_tables)

    def cells_call(cells, tile, near):
        buckets = cells.shape[0] // SENT * LANES
        scratch = [pltpu.VMEM((PARTS, 7 * LANES), bf16)] + [
            pltpu.VMEM((cell_count + top_count, LANES), f32),
            pltpu.VMEM((PARTS, 6 * LANES), bf16),
        ] * 2
        scratch += [
            pltpu.VMEM((buckets + TOP, LANES), f32),
            pltpu.VMEM((ROWS * buckets // LANES, LANES), f32),
            pltpu.VMEM((TOP // LANES * ROWS, LANES), f32),
            pltpu.VMEM((TOP // LANES * ROWS, LANES), f32),
        ]
        return pl.pallas_call(
            functools.partial(cells_kernel, near_count, cell_count, top_count),
            out_shape=work_shape,
            in_specs=[smem] * 2 + [vmem] * 3,
            out_specs=vmem,
            scratch_shapes=scratch,
            name="cell_force",
        )(work_lists, ess_all, cells, tile, near)

    near, tile = near_call(False, [])
    acc_one = sub_gather(cells_call(cells, tile, near), sub_count)
    flat_shape = jax.ShapeDtypeStruct((bucket_count * 8, LANES), f32)
    own_shape = jax.ShapeDtypeStruct(((bucket_count + 1) * 8, LANES), f32)

    def flat(values):
        return values.reshape(-1, LANES)

    own, places_two, base = pl.pallas_call(
        functools.partial(second_moments_kernel, sub_count),
        out_shape=(sent_shape, flat_shape, flat_shape),
        in_specs=[smem] * 2 + [vmem] * (4 + sub_count),
        out_specs=(vmem,) * 3,
        scratch_shapes=[pltpu.VMEM(own_shape.shape, f32)],
        name="second_moments",
    )(me_one, work_all, flat(ahead), flat(tiles), flat(speeds), tops_row, *acc_one)
    cells = exchange(own)
    near, tile = near_call(True, [*table_ahead, *acc_one])
    acc_two = sub_gather(cells_call(cells, tile, near), sub_count)
    speed_two = pl.pallas_call(
        functools.partial(final_kernel, sub_count),
        out_shape=flat_shape,
        in_specs=[smem] * 2 + [vmem] * (1 + sub_count),
        out_specs=vmem,
        scratch_shapes=[pltpu.VMEM(own_shape.shape, f32)],
        name="final_speeds",
    )(me_one, work_all, base, *acc_two)
    return (
        from_tiles(speed_two.reshape(-1, 8, LANES)),
        from_tiles(places_two.reshape(-1, 8, LANES)),
    )


def solution(mesh):
    both = ("dom", "sub")
    in_specs = (
        P(None, both),
        P(None, both),
        P(both),
        P(None, both),
        P(both),
        P(both),
        P(both, None),
        P(both, None),
        P(both, None),
        P("dom", "sub", None, None),
        P(both),
    )
    out_specs = (P(None, both), P(None, both))

    return jax.shard_map(body, mesh=mesh, in_specs=in_specs, out_specs=out_specs, check_vma=False)
```

```python
import functools

import jax
import jax.numpy as jnp
from jax import lax
from jax.experimental import pallas as pl
from jax.experimental.pallas import tpu as pltpu
from jax.sharding import PartitionSpec as P


TOP_SIDE = 16
TOP = TOP_SIDE**3
DT = 0.01
EPS = 0.0025
MASS_FLOOR = 0.5
LANES = 128
ROWS = 16
SENT = 11
LOWER = 256
PARTS = 4 * ROWS
CHUNKS = 1
CELL_CHUNK = 32
CELL_SPAN = 4


f32 = jnp.float32
bf16 = jnp.bfloat16


def other_slot(index, size, me):
    if size & (size - 1) == 0:
        return index ^ (me * size)
    return ((index // size) ^ me) * size + index % size


def to_tiles(three, one):
    flat = jnp.concatenate([three, one[None]], axis=0)
    count = flat.shape[1] // (2 * LANES)
    return flat.reshape(4, count, 2, LANES).transpose(1, 2, 0, 3).reshape(count, 8, LANES)


def from_tiles(tiles):
    count = tiles.shape[0]
    flat = tiles.reshape(count, 2, 4, LANES).transpose(2, 0, 1, 3).reshape(4, count * 2 * LANES)
    return flat[:3]


def sub_gather(block, sub_count, before_pass=None):
    parts = [None] * sub_count
    parts[0] = block
    for step in range(0, sub_count, 2):
        if step:
            parts[step] = lax.ppermute(block, "sub", [(i, i ^ step) for i in range(sub_count)])
            if before_pass is not None:
                parts[step], _ = lax.optimization_barrier((parts[step], before_pass))
    for step in range(0, sub_count, 2):
        parts[step + 1] = lax.ppermute(parts[step], "sub", [(i, i ^ 1) for i in range(sub_count)])
    return parts


def row_iota(shape=(8, LANES)):
    return lax.broadcasted_iota(jnp.int32, shape, 0)


def rounded(values):
    return values.astype(bf16).astype(f32)


def moments_of(get):
    weights = [get(0, 3), get(1, 3)]
    places = [[get(half, axis) for axis in range(3)] for half in range(2)]

    def total(one, two):
        return jnp.sum(one + two, axis=1, keepdims=True)

    mass = total(weights[0], weights[1])
    centre = [
        total(weights[0] * places[0][axis], weights[1] * places[1][axis]) / mass
        for axis in range(3)
    ]
    off = [[places[half][axis] - centre[axis] for axis in range(3)] for half in range(2)]
    woff = [[weights[half] * off[half][axis] for axis in range(3)] for half in range(2)]

    def second(a, b):
        return total(woff[0][a] * off[0][b], woff[1][a] * off[1][b])

    xx, yy, zz = second(0, 0), second(1, 1), second(2, 2)
    trace = xx + yy + zz
    return [mass] + centre + [
        3.0 * xx - trace,
        3.0 * yy - trace,
        3.0 * zz - trace,
        3.0 * second(0, 1),
        3.0 * second(0, 2),
        3.0 * second(1, 2),
    ]


def write_moments(columns, tops_row, out_ref, bucket_count):
    lane = lax.broadcasted_iota(jnp.int32, (bucket_count, LANES), 1)
    wide = jnp.zeros((bucket_count, LANES), f32)
    for q, column in enumerate(columns):
        wide = jnp.where(lane == q, column, wide)
    turned = jnp.transpose(wide)
    blocks = bucket_count // LANES
    for block in range(blocks):
        at = slice(block * LANES, (block + 1) * LANES)
        rows = jnp.concatenate([turned[:10, at], tops_row[:, at]], axis=0)
        for copy in range(out_ref.shape[0] // (blocks * SENT)):
            start = (copy * blocks + block) * SENT
            out_ref[start : start + SENT, :] = rows


def tile_rows(ref, row, bucket_count):
    return ref[pl.ds(row, bucket_count, stride=8), :]


def first_moments_kernel(tiles_ref, tops_ref, out_ref):
    bucket_count = tiles_ref.shape[0] // 8
    columns = moments_of(lambda half, row: tile_rows(tiles_ref, 4 * half + row, bucket_count))
    write_moments(columns, tops_ref[...], out_ref, bucket_count)


def spread_own(acc_refs, work_ref, me, own_ref, bucket_count):
    own_ref[...] = jnp.zeros_like(own_ref)
    count = work_ref.shape[1]
    for part, acc_ref in enumerate(acc_refs):

        @pl.loop(0, count, unroll=8 if count % 8 == 0 else 1)
        def _(i):
            bucket = work_ref[part, i] - me * bucket_count
            mine = jnp.logical_and(bucket >= 0, bucket < bucket_count)
            slot = pl.multiple_of(jnp.where(mine, bucket, bucket_count) * 8, 8)
            own_ref[pl.ds(slot, 8), :] = acc_ref[i]


def act_rows(tiles):
    count = tiles.shape[0] // 8
    wide = tiles.reshape(count, 8, LANES)
    row = lax.broadcasted_iota(jnp.int32, wide.shape, 1)
    first = jnp.broadcast_to(wide[:, 3:4, :], wide.shape)
    second = jnp.broadcast_to(wide[:, 7:8, :], wide.shape)
    return row % 4 == 3, jnp.where(row < 4, first, second), wide


def second_moments_kernel(
    sub_count, me_ref, work_ref, ahead_ref, tiles_ref, speeds_ref, tops_ref, *refs
):
    acc_refs, (out_ref, places_ref, base_ref, own_ref) = refs[:sub_count], refs[sub_count:]
    bucket_count = tiles_ref.shape[0] // 8
    spread_own(acc_refs, work_ref, me_ref[0], own_ref, bucket_count)

    @pl.loop(0, bucket_count // 8)
    def _(i):
        at = pl.ds(pl.multiple_of(i * 64, 64), 64)
        last, act, ahead = act_rows(ahead_ref[at, :])
        kick = DT * act * own_ref[at, :].reshape(8, 8, LANES)
        base_ref[at, :] = speeds_ref[at, :] + jnp.where(last, 0.0, kick).reshape(64, LANES)
        moved = ahead + DT * kick
        places = jnp.where(last, tiles_ref[at, :].reshape(8, 8, LANES), moved)
        places_ref[at, :] = places.reshape(64, LANES)

    columns = moments_of(lambda half, row: tile_rows(places_ref, 4 * half + row, bucket_count))
    write_moments(columns, tops_ref[...], out_ref, bucket_count)


def final_kernel(sub_count, me_ref, work_ref, base_ref, *refs):
    acc_refs, (out_ref, full_ref) = refs[:sub_count], refs[sub_count:]
    bucket_count = base_ref.shape[0] // 8
    full_ref[: bucket_count * 8, :] = base_ref[...]
    count = work_ref.shape[1]
    last = row_iota() % 4 == 3
    for part, acc_ref in enumerate(acc_refs):

        @pl.loop(0, count, unroll=8 if count % 8 == 0 else 1)
        def _(i):
            bucket = work_ref[part, i] - me_ref[0] * bucket_count
            mine = jnp.logical_and(bucket >= 0, bucket < bucket_count)
            tile = base_ref[pl.ds(pl.multiple_of(jnp.where(mine, bucket, 0) * 8, 8), 8), :]
            act = jnp.where(last, tile, 0.0)
            act = act + pltpu.roll(act, 7, 0) + pltpu.roll(act, 6, 0) + pltpu.roll(act, 5, 0)
            place = pl.ds(pl.multiple_of(jnp.where(mine, bucket, bucket_count) * 8, 8), 8)
            full_ref[place, :] = tile + (0.5 * DT) * act * acc_ref[i]

    out_ref[...] = full_ref[: bucket_count * 8, :]


def traceless(diag, cross):
    trace = diag[0] + diag[1] + diag[2]
    return [3.0 * d - trace for d in diag] + [3.0 * c for c in cross]


def outer(first, second):
    return (
        [first[a] * second[a] for a in range(3)],
        [first[0] * second[1], first[0] * second[2], first[1] * second[2]],
    )


def in_parts(values):
    high, middle, low = three(values)
    return jnp.concatenate([high, middle, low, jnp.ones_like(values)], axis=0)


def build_rows(cells_ref, rows_ref, raw_ref, sums_ref, tops_ref):
    blocks = cells_ref.shape[0] // SENT
    uppers = TOP // LOWER
    sides = LOWER // LANES
    for block in range(blocks):
        start = block * SENT
        if start + ROWS <= cells_ref.shape[0]:
            turned = cells_ref[start : start + ROWS, :]
        else:
            turned = jnp.concatenate(
                [cells_ref[start : start + SENT, :], jnp.zeros((ROWS - SENT, LANES), f32)], axis=0
            )
        rows_ref[block * LANES : (block + 1) * LANES, :PARTS] = jnp.transpose(in_parts(turned))
    side = TOP_SIDE

    def sent(q):
        return cells_ref[pl.ds(q, blocks, stride=SENT), :]

    top_id = sent(10).astype(jnp.int32)
    index = [top_id // (side * side), top_id // side % side, top_id % side]
    mass = sent(0)
    delta = [sent(1 + a) - (index[a].astype(f32) + 0.5) / side for a in range(3)]
    first = [mass * delta[a] for a in range(3)]
    lifted = traceless(*outer(first, delta))
    raw = [mass] + first + [sent(4 + k) + lifted[k] for k in range(6)]
    for q in range(ROWS):
        raw_ref[q * blocks : (q + 1) * blocks, :] = raw[q] if q < 10 else jnp.zeros_like(mass)
    sums_ref[...] = jnp.zeros_like(sums_ref)
    pair = 2 if blocks % 2 == 0 else 1

    @pl.loop(0, blocks // pair)
    def _(step):
        top, values = [], []
        for part in range(pair):
            block = step * pair + part
            top.append(cells_ref[pl.ds(block * SENT + 10, 1), :])
            values.append(raw_ref[pl.ds(block, ROWS, stride=blocks), :])
        top = jnp.concatenate(top, axis=1).astype(jnp.int32)
        values = jnp.concatenate(values, axis=1)
        high = values.astype(bf16)
        low = (values - high.astype(f32)).astype(bf16)
        width = top.shape[1]
        upper = jnp.broadcast_to(top // LOWER, (ROWS, width))
        lower = jnp.broadcast_to(top % LOWER, (LOWER, width))
        match = lax.broadcasted_iota(jnp.int32, (LOWER, width), 0) == lower
        picks = jnp.where(match, 1.0, 0.0).astype(bf16)
        empty = jnp.zeros_like(high)
        parts = []
        for piece in (high, low):
            left = jnp.concatenate(
                [jnp.where(upper == u, piece, empty) for u in range(uppers)], axis=0
            )
            parts.append(
                lax.dot_general(left, picks, (((1,), (1,)), ((), ())), preferred_element_type=f32)
            )
        both = parts[0] + parts[1]
        for side_at in range(sides):
            rows = slice(side_at * uppers * ROWS, (side_at + 1) * uppers * ROWS)
            sums_ref[rows, :] += both[:, side_at * LANES : (side_at + 1) * LANES]

    cell = lax.broadcasted_iota(jnp.int32, (uppers, LOWER), 0) * LOWER
    cell = cell + lax.broadcasted_iota(jnp.int32, (uppers, LOWER), 1)
    index = [cell // (side * side), cell // side % side, cell % side]

    def summed(q):
        return jnp.concatenate(
            [
                sums_ref[pl.ds(side_at * uppers * ROWS + q, uppers, stride=ROWS), :]
                for side_at in range(sides)
            ],
            axis=1,
        )

    mass = summed(0)
    inverse = 1.0 / jnp.maximum(mass, MASS_FLOOR)
    first = [summed(1 + a) for a in range(3)]
    shift = [first[a] * inverse for a in range(3)]
    lowered = traceless(*outer(first, shift))
    tops = (
        [mass]
        + [(index[a].astype(f32) + 0.5) / side + shift[a] for a in range(3)]
        + [summed(4 + k) - lowered[k] for k in range(6)]
    )
    for q in range(10):
        for side_at in range(sides):
            at = pl.ds(side_at * uppers * ROWS + q, uppers, stride=ROWS)
            tops_ref[at, :] = tops[q][:, side_at * LANES : (side_at + 1) * LANES]
    for u in range(uppers):
        for side_at in range(sides):
            start = blocks * LANES + u * LOWER + side_at * LANES
            rows = (side_at * uppers + u) * ROWS
            rows_ref[start : start + LANES, :PARTS] = jnp.transpose(
                in_parts(tops_ref[rows : rows + ROWS, :])
            )


def cell_terms(off, mass, quad, sums):
    dist = off[0] * off[0] + off[1] * off[1] + off[2] * off[2] + EPS
    inv = lax.rsqrt(dist)
    inv_two = inv * inv
    inv_five = inv_two * inv_two * inv
    along = [
        quad[0] * off[0] + quad[3] * off[1] + quad[4] * off[2],
        quad[3] * off[0] + quad[1] * off[1] + quad[5] * off[2],
        quad[4] * off[0] + quad[5] * off[1] + quad[2] * off[2],
    ]
    both = off[0] * along[0] + off[1] * along[1] + off[2] * along[2]
    radial = mass * dist + 2.5 * both * inv_two
    for a in range(3):
        sums[a] += (along[a] - radial * off[a]) * inv_five


def with_norm(values, extra, scale, last):
    squares = jnp.where(last, 0.0, values * values)
    norm = pltpu.roll(squares, 1, 0) + pltpu.roll(squares, 2, 0) + pltpu.roll(squares, 3, 0)
    return jnp.where(last, norm + extra, scale * values)


def three(values):
    high = rounded(values)
    rest = values - high
    middle = rounded(rest)
    return high, middle, rest - middle


def prepare_near(tile, sources, masses, left_ref, right_ref, pull_ref, target_ref):
    row = row_iota()
    last = row % 4 == 3
    front = row < 4
    mean = jnp.sum(tile, axis=1, keepdims=True)
    mean = jnp.broadcast_to(mean, (8, LANES))
    centre = jnp.where(last, 0.0, (mean + pltpu.roll(mean, 4, 0)) * (0.5 / LANES))
    target = tile - centre
    target_ref[...] = target
    high, middle, low = three(with_norm(target, EPS, -2.0, last))
    plain = jnp.where(last, 1.0, high)
    blocks = [plain, plain, plain, jnp.where(last, high, middle), middle, low]
    turned = [pltpu.roll(block, 4, 0) for block in blocks]
    first = [jnp.where(front, b, t) for b, t in zip(blocks, turned)]
    second = [jnp.where(front, t, b) for b, t in zip(blocks, turned)]
    for half in range(2):
        keep = front if half == 0 else jnp.logical_not(front)
        for side, parts in enumerate((first, second)):
            right_ref[half, :, side * LANES : (side + 1) * LANES] = jnp.concatenate(
                [jnp.where(keep, part, 0.0) for part in parts], axis=0
            ).astype(bf16)
    for k, (source, weights) in enumerate(zip(sources, masses)):
        at = slice(k * LANES, (k + 1) * LANES)
        place = source - centre
        high, middle, low = three(with_norm(place, 0.0, 1.0, last))
        high_one = jnp.where(last, 1.0, high)
        middle_one = jnp.where(last, 1.0, middle)
        stack = jnp.concatenate([high, middle, low, high_one, middle_one, high_one], axis=0)
        left_ref[at, :] = jnp.transpose(stack).astype(bf16)
        mass = jnp.where(last, weights, 0.0)
        mass = mass + pltpu.roll(mass, 7, 0) + pltpu.roll(mass, 6, 0) + pltpu.roll(mass, 5, 0)
        moved = mass * place
        moved_high, mass_high = rounded(moved), rounded(mass)
        pull_ref[:, at] = jnp.concatenate(
            [moved_high, moved - moved_high, mass_high, mass - mass_high], axis=0
        ).astype(bf16)


def near_distances(operand, start, width):
    left_ref, right_ref = operand[:2]
    left = left_ref[start : start + width, :]
    return [jnp.dot(left, right_ref[half], preferred_element_type=f32) for half in range(2)]


def near_pulls(operand, start, width, dist, total):
    pull = operand[2][:, start : start + width]
    weight = [lax.rsqrt((d * d * d).astype(bf16)) for d in dist]
    for half in range(2):
        part = jnp.dot(pull, weight[half], preferred_element_type=f32)
        total[half] = part if total[half] is None else total[half] + part


def near_result(target, total):
    row = row_iota()
    last = row % 4 == 3
    front = row < 4

    def fold(start):
        parts = [t[start : start + 8, :] + t[start + 8 : start + 16, :] for t in total]
        sides = []
        for side in range(2):
            at = slice(side * LANES, (side + 1) * LANES)
            mixed = jnp.where(front, parts[0][:, at], parts[1][:, at])
            sides.append(mixed + pltpu.roll(mixed, 4, 0))
        return jnp.where(front, sides[0], sides[1])

    return jnp.where(last, 0.0, fold(0) - target * fold(16))


def near_kernel(second, sub_count, bucket_count, near_count, me_ref, work_ref, list_ref, *refs):
    refs = list(refs)
    tables = [refs.pop(0) for _ in range(sub_count * CHUNKS)]
    if second:
        table_refs = [refs.pop(0) for _ in range(sub_count)]
        acc_refs = [refs.pop(0) for _ in range(sub_count)]
    out_ref, tile_ref = refs[:2]
    refs = refs[2:]
    group_ref, sem = refs[:2]
    operands = [refs[2 + 4 * k : 6 + 4 * k] for k in range(8)]
    me = me_ref[0]
    mass_ref = group_ref
    if second:
        mass_ref, acc_ref = refs[2 + 4 * 8 :]
    piece = bucket_count // CHUNKS
    copies = [
        pltpu.make_async_copy(ref, mass_ref.at[pl.ds(k * piece, piece)], sem.at[k])
        for k, ref in enumerate(tables)
    ]
    if second:
        copies += [
            pltpu.make_async_copy(
                table_refs[k],
                group_ref.at[pl.ds(k * bucket_count, bucket_count)],
                sem.at[len(tables) + k],
            )
            for k in range(sub_count)
        ]
        copies += [
            pltpu.make_async_copy(acc_refs[k], acc_ref.at[k], sem.at[len(tables) + sub_count + k])
            for k in range(sub_count)
        ]
    for copy in copies:
        copy.start()
    for copy in copies:
        copy.wait()
    if second:
        last = row_iota() % 4 == 3
        for part in range(sub_count):

            @pl.loop(0, work_ref.shape[1], unroll=4)
            def _(i):
                slot = other_slot(work_ref[part, i], bucket_count, me)
                tile = group_ref[slot]
                act = jnp.where(last, tile, 0.0)
                act = act + pltpu.roll(act, 7, 0) + pltpu.roll(act, 6, 0) + pltpu.roll(act, 5, 0)
                group_ref[slot] = tile + (DT * DT) * act * acc_ref[part, i]

    def prepare(i, slot):
        tile = group_ref[other_slot(work_ref[0, i], bucket_count, me)]
        tile_ref[i] = tile
        slots = [list_ref[i, k] for k in range(near_count)]
        prepare_near(
            tile, [group_ref[n] for n in slots], [mass_ref[n] for n in slots], *operands[slot]
        )

    count = work_ref.shape[1]
    span = 8
    width = 2 * LANES
    rows = near_count * LANES
    prepare(0, 0)

    @pl.loop(0, pl.cdiv(count, span))
    def _(block):
        steps = [(part, start) for part in range(span) for start in range(0, rows, width)]
        first = block * span
        totals = {}

        def finish(part, start, dist):
            near_pulls(operands[part], start, width, dist, totals[part])
            if start + width == rows:
                target = operands[part][3][...]
                out_ref[jnp.minimum(first + part, count - 1)] = near_result(target, totals[part])

        pending = None
        for part, start in steps:
            if start == 0:
                totals[part] = [None, None]
            if start == width and part + 1 < span:
                prepare(jnp.minimum(first + part + 1, count - 1), part + 1)
            dist = near_distances(operands[part], start, width)
            if pending is not None:
                finish(*pending)
            pending = (part, start, dist)
        prepare(jnp.minimum(first + span, count - 1), 0)
        finish(*pending)


def splat_operand():
    shape = (PARTS, 7 * LANES)
    row = lax.broadcasted_iota(jnp.int32, shape, 0)
    number = lax.broadcasted_iota(jnp.int32, shape, 1) // LANES
    wanted = jnp.where(number == 0, 0, number + 3)
    keep = jnp.logical_and(row % ROWS == wanted, row < 3 * ROWS)
    return jnp.where(keep, 1.0, 0.0).astype(bf16)


def centre_operand():
    shape = (3 * ROWS, 6 * LANES)
    row = lax.broadcasted_iota(jnp.int32, shape, 0)
    number = lax.broadcasted_iota(jnp.int32, shape, 1) // (2 * LANES)
    return jnp.where(row % ROWS == number + 1, -1.0, 0.0).astype(bf16)


def cells_kernel(
    near_count,
    cell_count,
    top_count,
    list_ref,
    ess_ref,
    cells_ref,
    tile_ref,
    near_ref,
    out_ref,
    splat_ref,
    *slots,
):
    rows_ref = slots[4]
    build_rows(cells_ref, *slots[4:])
    splat_ref[...] = splat_operand()
    for side in range(2):
        slots[2 * side + 1][: 3 * ROWS, :] = centre_operand()
    count = tile_ref.shape[0]
    total = cell_count + top_count

    def pick_rows(i, slot, start, stop):
        picked_ref = slots[2 * slot]
        for k in range(start, stop):
            index = list_ref[i, near_count + k]
            if k < cell_count:
                index = ess_ref[index]
            picked_ref[pl.ds(k, 1), :] = rows_ref[pl.ds(index, 1), :]

    def place(i, slot):
        places_ref = slots[2 * slot + 1]
        parts = three(tile_ref[i])
        row = row_iota((ROWS, LANES))
        for half in range(2):
            for a in range(3):
                at = 4 * half + a
                spread = [jnp.broadcast_to(p[at : at + 1, :], (ROWS, LANES)) for p in parts]
                value = jnp.where(
                    row == 0,
                    spread[0],
                    jnp.where(row == 1, spread[1], jnp.where(row == 2, spread[2], 0.0)),
                )
                lanes = slice((2 * a + half) * LANES, (2 * a + half + 1) * LANES)
                places_ref[3 * ROWS :, lanes] = value.astype(bf16)

    def spread_cells(slot, start):
        picked_ref, places_ref = slots[2 * slot : 2 * slot + 2]
        left = picked_ref[start : start + CELL_CHUNK, :PARTS].astype(bf16)
        return (
            jnp.dot(left, splat_ref[...], preferred_element_type=f32),
            jnp.dot(left, places_ref[...], preferred_element_type=f32),
        )

    def finish(i, sums):
        row = row_iota()
        result = near_ref[i]
        for half in range(2):
            for a in range(3):
                value = jnp.sum(sums[half][a], axis=0, keepdims=True)
                value = jnp.broadcast_to(value, (8, LANES))
                result += jnp.where(row == 4 * half + a, value, 0.0)
        out_ref[i] = result

    pick_rows(0, 0, 0, total)
    place(0, 0)
    chunks = range(0, total, CELL_CHUNK)
    early = (len(chunks) - 1) * CELL_CHUNK // 8
    share = -(-total // early)

    @pl.loop(0, pl.cdiv(count, CELL_SPAN))
    def _(block):
        item = [jnp.minimum(CELL_SPAN * block + k, count - 1) for k in range(CELL_SPAN + 1)]
        waiting = spread_cells(0, 0)
        for step in range(CELL_SPAN):
            slot = step % 2
            sums = [[jnp.zeros((8, LANES), f32) for _ in range(3)] for _ in range(2)]
            done = 0
            place(item[step + 1], 1 - slot)
            for start in chunks:
                splats, offs = waiting
                if start + CELL_CHUNK < total:
                    waiting = spread_cells(slot, start + CELL_CHUNK)
                elif step + 1 < CELL_SPAN:
                    waiting = spread_cells(1 - slot, 0)
                for group in range(CELL_CHUNK // 8):
                    rows = slice(8 * group, 8 * group + 8)
                    number = [splats[rows, q * LANES : (q + 1) * LANES] for q in range(7)]
                    for half in range(2):
                        off = [
                            offs[rows, (2 * a + half) * LANES : (2 * a + half + 1) * LANES]
                            for a in range(3)
                        ]
                        cell_terms(off, number[0], number[1:], sums[half])
                    if done < total:
                        pick_rows(item[step + 1], 1 - slot, done, min(done + share, total))
                        done += share
            finish(item[step], sums)


def body(
    positions,
    velocities,
    masses,
    accel_prev,
    active,
    bucket_top,
    near_list,
    cell_list,
    top_list,
    essential,
    work,
):
    bucket_count = bucket_top.shape[0]
    sub_count = lax.axis_size("sub")
    dom_count = lax.axis_size("dom")
    me = lax.axis_index("sub").astype(jnp.int32)
    group_buckets = sub_count * bucket_count
    device_count = sub_count * dom_count
    near_count, cell_count, top_count = near_list.shape[1], cell_list.shape[1], top_list.shape[1]
    work_count = work.shape[0]
    vmem = pl.BlockSpec(memory_space=pltpu.VMEM)
    smem = pl.BlockSpec(memory_space=pltpu.SMEM)
    anywhere = pl.BlockSpec(memory_space=pl.ANY)
    work_shape = jax.ShapeDtypeStruct((work_count, 8, LANES), f32)
    sent_shape = jax.ShapeDtypeStruct((device_count * bucket_count // LANES * SENT, LANES), f32)

    activity = active.astype(f32)
    half_speed = velocities + 0.5 * DT * activity * accel_prev
    places = positions + DT * half_speed
    tiles = to_tiles(places, masses)
    places, half_speed, activity, _ = lax.optimization_barrier(
        (places, half_speed, activity, tiles)
    )
    ahead = to_tiles(places + DT * half_speed, activity)
    speeds = to_tiles(half_speed, activity)

    tops_row = bucket_top.astype(f32)[None]

    own = pl.pallas_call(
        first_moments_kernel,
        out_shape=sent_shape,
        in_specs=[vmem] * 2,
        out_specs=vmem,
        compiler_params=pltpu.CompilerParams(vmem_limit_bytes=20 << 20),
        name="first_moments",
    )(tiles.reshape(-1, LANES), tops_row)

    def exchange(rows):
        wide = rows.reshape(device_count, -1)
        got = lax.all_to_all(wide, ("dom", "sub"), split_axis=0, concat_axis=0, tiled=True)
        return got.reshape(-1, LANES)

    cells = exchange(own)
    near_list, cell_list, top_list, essential, work, _ = lax.optimization_barrier(
        (near_list, cell_list, top_list, essential, work, own)
    )

    def as_rows(values):
        return jnp.pad(values, (0, -values.shape[0] % LANES)).reshape(-1, LANES)

    lists = jnp.concatenate([near_list, cell_list, top_list], axis=1)
    lists = jnp.pad(lists, ((0, 0), (0, -lists.shape[1] % LANES)))
    width = lists.shape[1]
    wanted = essential.reshape(dom_count, -1) + (
        jnp.arange(dom_count, dtype=jnp.int32) * group_buckets
    )[:, None]
    ess_size = wanted.size
    list_rows = bucket_count * width // LANES
    ess_rows = -(-ess_size // LANES)
    sent = jnp.concatenate(
        [lists.reshape(-1, LANES), as_rows(wanted.reshape(-1)), as_rows(work)], axis=0
    )
    sent_rows = sent.shape[0]
    sent = jnp.pad(sent, ((0, -sent_rows % 8), (0, 0)))
    all_rows = jnp.stack(sub_gather(sent, sub_count))
    ess_all = all_rows[:, list_rows : list_rows + ess_rows].reshape(sub_count, -1)
    ess_all = ess_all[:, :ess_size].reshape(-1)
    work_all = all_rows[:, list_rows + ess_rows : sent_rows].reshape(sub_count, -1)
    work_all = work_all[:, :work_count]
    mine = other_slot(work, bucket_count, me)
    if width == LANES:
        index = mine // bucket_count * sent.shape[0] + mine % bucket_count
        work_lists = jnp.take(all_rows.reshape(-1, LANES), index, axis=0)
    else:
        list_table = all_rows[:, :list_rows].reshape(group_buckets, width)
        work_lists = jnp.take(list_table, mine, axis=0)
    column = jnp.arange(width)[None]
    work_lists = jnp.where(
        column < near_count,
        other_slot(work_lists, bucket_count, me),
        jnp.where(
            column < near_count + cell_count,
            other_slot(work_lists, ess_size, me),
            work_lists + device_count * bucket_count,
        ),
    )
    piece = bucket_count // CHUNKS
    pieces = [sub_gather(tiles[c * piece : (c + 1) * piece], sub_count, work_lists) for c in range(CHUNKS)]
    table = [pieces[c][k] for k in range(sub_count) for c in range(CHUNKS)]
    ahead_sent, _ = lax.optimization_barrier((ahead, table))
    table_ahead = sub_gather(ahead_sent, sub_count)

    me_one = me[None]

    def near_call(second, extra_tables):
        operand = [
            pltpu.VMEM((near_count * LANES, 48), bf16),
            pltpu.VMEM((2, 48, 2 * LANES), bf16),
            pltpu.VMEM((32, near_count * LANES), bf16),
            pltpu.VMEM((8, LANES), f32),
        ]
        scratch = [
            pltpu.VMEM((group_buckets, 8, LANES), f32),
            pltpu.SemaphoreType.DMA(((2 + CHUNKS) * sub_count,)),
        ] + operand * 8
        specs = [smem] * 3 + [anywhere] * (sub_count * CHUNKS)
        if second:
            specs += [anywhere] * (2 * sub_count)
            scratch += [
                pltpu.VMEM((group_buckets, 8, LANES), f32),
                pltpu.VMEM((sub_count, work_count, 8, LANES), f32),
            ]
        return pl.pallas_call(
            functools.partial(near_kernel, second, sub_count, bucket_count, near_count),
            out_shape=(work_shape, work_shape),
            in_specs=specs,
            out_specs=(vmem, vmem),
            scratch_shapes=scratch,
            compiler_params=pltpu.CompilerParams(vmem_limit_bytes=20 << 20),
            name="near_second" if second else "near_first",
        )(me_one, work_all, work_lists, *table, *extra_tables)

    def cells_call(cells, tile, near):
        buckets = cells.shape[0] // SENT * LANES
        scratch = [pltpu.VMEM((PARTS, 7 * LANES), bf16)] + [
            pltpu.VMEM((cell_count + top_count, LANES), f32),
            pltpu.VMEM((PARTS, 6 * LANES), bf16),
        ] * 2
        scratch += [
            pltpu.VMEM((buckets + TOP, LANES), f32),
            pltpu.VMEM((ROWS * buckets // LANES, LANES), f32),
            pltpu.VMEM((TOP // LANES * ROWS, LANES), f32),
            pltpu.VMEM((TOP // LANES * ROWS, LANES), f32),
        ]
        return pl.pallas_call(
            functools.partial(cells_kernel, near_count, cell_count, top_count),
            out_shape=work_shape,
            in_specs=[smem] * 2 + [vmem] * 3,
            out_specs=vmem,
            scratch_shapes=scratch,
            name="cell_force",
        )(work_lists, ess_all, cells, tile, near)

    near, tile = near_call(False, [])
    acc_one = sub_gather(cells_call(cells, tile, near), sub_count)
    flat_shape = jax.ShapeDtypeStruct((bucket_count * 8, LANES), f32)
    own_shape = jax.ShapeDtypeStruct(((bucket_count + 1) * 8, LANES), f32)

    def flat(values):
        return values.reshape(-1, LANES)

    own, places_two, base = pl.pallas_call(
        functools.partial(second_moments_kernel, sub_count),
        out_shape=(sent_shape, flat_shape, flat_shape),
        in_specs=[smem] * 2 + [vmem] * (4 + sub_count),
        out_specs=(vmem,) * 3,
        scratch_shapes=[pltpu.VMEM(own_shape.shape, f32)],
        compiler_params=pltpu.CompilerParams(vmem_limit_bytes=20 << 20),
        name="second_moments",
    )(me_one, work_all, flat(ahead), flat(tiles), flat(speeds), tops_row, *acc_one)
    cells = exchange(own)
    near, tile = near_call(True, [*table_ahead, *acc_one])
    acc_two = sub_gather(cells_call(cells, tile, near), sub_count)
    speed_two = pl.pallas_call(
        functools.partial(final_kernel, sub_count),
        out_shape=flat_shape,
        in_specs=[smem] * 2 + [vmem] * (1 + sub_count),
        out_specs=vmem,
        scratch_shapes=[pltpu.VMEM(own_shape.shape, f32)],
        compiler_params=pltpu.CompilerParams(vmem_limit_bytes=20 << 20),
        name="final_speeds",
    )(me_one, work_all, base, *acc_two)
    return (
        from_tiles(speed_two.reshape(-1, 8, LANES)),
        from_tiles(places_two.reshape(-1, 8, LANES)),
    )


def solution(mesh):
    both = ("dom", "sub")
    in_specs = (
        P(None, both),
        P(None, both),
        P(both),
        P(None, both),
        P(both),
        P(both),
        P(both, None),
        P(both, None),
        P(both, None),
        P("dom", "sub", None, None),
        P(both),
    )
    out_specs = (P(None, both), P(None, both))

    return jax.shard_map(body, mesh=mesh, in_specs=in_specs, out_specs=out_specs, check_vma=False)
```

```python
import functools

import jax
import jax.numpy as jnp
from jax import lax
from jax.experimental import pallas as pl
from jax.experimental.pallas import tpu as pltpu
from jax.sharding import PartitionSpec as P


TOP_SIDE = 16
TOP = TOP_SIDE**3
DT = 0.01
EPS = 0.0025
MASS_FLOOR = 0.5
LANES = 128
ROWS = 16
SENT = 11
LOWER = 256
PARTS = 80
CHUNKS = 1
CELL_CHUNK = 48
CELL_SPAN = 8


f32 = jnp.float32
bf16 = jnp.bfloat16


def other_slot(index, size, me):
    if size & (size - 1) == 0:
        return index ^ (me * size)
    return ((index // size) ^ me) * size + index % size


def to_tiles(three, one):
    flat = jnp.concatenate([three, one[None]], axis=0)
    count = flat.shape[1] // (2 * LANES)
    return flat.reshape(4, count, 2, LANES).transpose(1, 2, 0, 3).reshape(count, 8, LANES)


def from_tiles(tiles):
    count = tiles.shape[0]
    flat = tiles.reshape(count, 2, 4, LANES).transpose(2, 0, 1, 3).reshape(4, count * 2 * LANES)
    return flat[:3]


def sub_gather(block, sub_count, before_pass=None):
    parts = [None] * sub_count
    parts[0] = block
    for step in range(0, sub_count, 2):
        if step:
            parts[step] = lax.ppermute(block, "sub", [(i, i ^ step) for i in range(sub_count)])
            if before_pass is not None:
                parts[step], _ = lax.optimization_barrier((parts[step], before_pass))
    for step in range(0, sub_count, 2):
        parts[step + 1] = lax.ppermute(parts[step], "sub", [(i, i ^ 1) for i in range(sub_count)])
    return parts


def row_iota(shape=(8, LANES)):
    return lax.broadcasted_iota(jnp.int32, shape, 0)


def rounded(values):
    return values.astype(bf16).astype(f32)


def moments_of(get):
    weights = [get(0, 3), get(1, 3)]
    places = [[get(half, axis) for axis in range(3)] for half in range(2)]

    def total(one, two):
        return jnp.sum(one + two, axis=1, keepdims=True)

    mass = total(weights[0], weights[1])
    centre = [
        total(weights[0] * places[0][axis], weights[1] * places[1][axis]) / mass
        for axis in range(3)
    ]
    off = [[places[half][axis] - centre[axis] for axis in range(3)] for half in range(2)]
    woff = [[weights[half] * off[half][axis] for axis in range(3)] for half in range(2)]

    def second(a, b):
        return total(woff[0][a] * off[0][b], woff[1][a] * off[1][b])

    xx, yy, zz = second(0, 0), second(1, 1), second(2, 2)
    trace = xx + yy + zz
    return [mass] + centre + [
        3.0 * xx - trace,
        3.0 * yy - trace,
        3.0 * zz - trace,
        3.0 * second(0, 1),
        3.0 * second(0, 2),
        3.0 * second(1, 2),
    ]


def write_moments(columns, tops_row, out_ref, bucket_count):
    lane = lax.broadcasted_iota(jnp.int32, (bucket_count, LANES), 1)
    wide = jnp.zeros((bucket_count, LANES), f32)
    for q, column in enumerate(columns):
        wide = jnp.where(lane == q, column, wide)
    turned = jnp.transpose(wide)
    blocks = bucket_count // LANES
    for block in range(blocks):
        at = slice(block * LANES, (block + 1) * LANES)
        rows = jnp.concatenate([turned[:10, at], tops_row[:, at]], axis=0)
        for copy in range(out_ref.shape[0] // (blocks * SENT)):
            start = (copy * blocks + block) * SENT
            out_ref[start : start + SENT, :] = rows


def tile_rows(ref, row, bucket_count):
    return ref[pl.ds(row, bucket_count, stride=8), :]


def first_moments_kernel(tiles_ref, tops_ref, out_ref):
    bucket_count = tiles_ref.shape[0] // 8
    columns = moments_of(lambda half, row: tile_rows(tiles_ref, 4 * half + row, bucket_count))
    write_moments(columns, tops_ref[...], out_ref, bucket_count)


def spread_own(acc_refs, work_ref, me, own_ref, bucket_count):
    own_ref[...] = jnp.zeros_like(own_ref)
    count = work_ref.shape[1]
    for part, acc_ref in enumerate(acc_refs):

        @pl.loop(0, count, unroll=8 if count % 8 == 0 else 1)
        def _(i):
            bucket = work_ref[part, i] - me * bucket_count
            mine = jnp.logical_and(bucket >= 0, bucket < bucket_count)
            slot = pl.multiple_of(jnp.where(mine, bucket, bucket_count) * 8, 8)
            own_ref[pl.ds(slot, 8), :] = acc_ref[i]


def act_rows(tiles):
    count = tiles.shape[0] // 8
    wide = tiles.reshape(count, 8, LANES)
    row = lax.broadcasted_iota(jnp.int32, wide.shape, 1)
    first = jnp.broadcast_to(wide[:, 3:4, :], wide.shape)
    second = jnp.broadcast_to(wide[:, 7:8, :], wide.shape)
    return row % 4 == 3, jnp.where(row < 4, first, second), wide


def second_moments_kernel(
    sub_count, me_ref, work_ref, ahead_ref, tiles_ref, speeds_ref, tops_ref, *refs
):
    acc_refs, (out_ref, places_ref, base_ref, own_ref) = refs[:sub_count], refs[sub_count:]
    bucket_count = tiles_ref.shape[0] // 8
    spread_own(acc_refs, work_ref, me_ref[0], own_ref, bucket_count)

    @pl.loop(0, bucket_count // 8)
    def _(i):
        at = pl.ds(pl.multiple_of(i * 64, 64), 64)
        last, act, ahead = act_rows(ahead_ref[at, :])
        kick = DT * act * own_ref[at, :].reshape(8, 8, LANES)
        base_ref[at, :] = speeds_ref[at, :] + jnp.where(last, 0.0, kick).reshape(64, LANES)
        moved = ahead + DT * kick
        places = jnp.where(last, tiles_ref[at, :].reshape(8, 8, LANES), moved)
        places_ref[at, :] = places.reshape(64, LANES)

    columns = moments_of(lambda half, row: tile_rows(places_ref, 4 * half + row, bucket_count))
    write_moments(columns, tops_ref[...], out_ref, bucket_count)


def final_kernel(sub_count, me_ref, work_ref, base_ref, *refs):
    acc_refs, (out_ref, full_ref) = refs[:sub_count], refs[sub_count:]
    bucket_count = base_ref.shape[0] // 8
    full_ref[: bucket_count * 8, :] = base_ref[...]
    count = work_ref.shape[1]
    last = row_iota() % 4 == 3
    for part, acc_ref in enumerate(acc_refs):

        @pl.loop(0, count, unroll=8 if count % 8 == 0 else 1)
        def _(i):
            bucket = work_ref[part, i] - me_ref[0] * bucket_count
            mine = jnp.logical_and(bucket >= 0, bucket < bucket_count)
            tile = base_ref[pl.ds(pl.multiple_of(jnp.where(mine, bucket, 0) * 8, 8), 8), :]
            act = jnp.where(last, tile, 0.0)
            act = act + pltpu.roll(act, 7, 0) + pltpu.roll(act, 6, 0) + pltpu.roll(act, 5, 0)
            place = pl.ds(pl.multiple_of(jnp.where(mine, bucket, bucket_count) * 8, 8), 8)
            full_ref[place, :] = tile + (0.5 * DT) * act * acc_ref[i]

    out_ref[...] = full_ref[: bucket_count * 8, :]


def traceless(diag, cross):
    trace = diag[0] + diag[1] + diag[2]
    return [3.0 * d - trace for d in diag] + [3.0 * c for c in cross]


def outer(first, second):
    return (
        [first[a] * second[a] for a in range(3)],
        [first[0] * second[1], first[0] * second[2], first[1] * second[2]],
    )


def write_cells(cells_ref, start, count, mass, centre, quad):
    turned = [
        quad[0] * centre[0] + quad[3] * centre[1] + quad[4] * centre[2],
        quad[3] * centre[0] + quad[1] * centre[1] + quad[5] * centre[2],
        quad[4] * centre[0] + quad[5] * centre[1] + quad[2] * centre[2],
    ]
    zero = jnp.zeros_like(mass)
    values = quad + [zero, zero] + centre + turned + [mass, jnp.ones_like(mass)]
    for q, value in enumerate(values):
        cells_ref[pl.ds(start * ROWS + q, count, stride=ROWS), :] = value


def in_parts(values):
    high, middle, low = three(values)
    one = row_iota() == 7
    tail = [jnp.where(one, 1.0, part[8:]) for part in (high, middle, low)]
    quad = [part[:8] for part in (high, high, high, middle, middle, low)]
    return jnp.concatenate(quad + tail + [jnp.zeros((8, LANES), f32)], axis=0)


def build_rows(sent_ref, rows_ref, raw_ref, sums_ref, cells_ref):
    blocks = sent_ref.shape[0] // SENT
    uppers = TOP // LOWER
    sides = LOWER // LANES
    side = TOP_SIDE

    def sent(q):
        return sent_ref[pl.ds(q, blocks, stride=SENT), :]

    top_id = sent(10).astype(jnp.int32)
    index = [top_id // (side * side), top_id // side % side, top_id % side]
    mass = sent(0)
    centre = [sent(1 + a) for a in range(3)]
    quad = [sent(4 + k) for k in range(6)]
    write_cells(cells_ref, 0, blocks, mass, centre, quad)
    delta = [centre[a] - (index[a].astype(f32) + 0.5) / side for a in range(3)]
    first = [mass * delta[a] for a in range(3)]
    lifted = traceless(*outer(first, delta))
    raw = [mass] + first + [quad[k] + lifted[k] for k in range(6)]
    for q in range(ROWS):
        raw_ref[q * blocks : (q + 1) * blocks, :] = raw[q] if q < 10 else jnp.zeros_like(mass)
    sums_ref[...] = jnp.zeros_like(sums_ref)
    pair = 2 if blocks % 2 == 0 else 1

    @pl.loop(0, blocks // pair)
    def _(step):
        top, values = [], []
        for part in range(pair):
            block = step * pair + part
            top.append(sent_ref[pl.ds(block * SENT + 10, 1), :])
            values.append(raw_ref[pl.ds(block, ROWS, stride=blocks), :])
        top = jnp.concatenate(top, axis=1).astype(jnp.int32)
        values = jnp.concatenate(values, axis=1)
        high = values.astype(bf16)
        low = (values - high.astype(f32)).astype(bf16)
        width = top.shape[1]
        upper = jnp.broadcast_to(top // LOWER, (ROWS, width))
        lower = jnp.broadcast_to(top % LOWER, (LOWER, width))
        match = lax.broadcasted_iota(jnp.int32, (LOWER, width), 0) == lower
        picks = jnp.where(match, 1.0, 0.0).astype(bf16)
        empty = jnp.zeros_like(high)
        parts = []
        for piece in (high, low):
            left = jnp.concatenate(
                [jnp.where(upper == u, piece, empty) for u in range(uppers)], axis=0
            )
            parts.append(
                lax.dot_general(left, picks, (((1,), (1,)), ((), ())), preferred_element_type=f32)
            )
        both = parts[0] + parts[1]
        for side_at in range(sides):
            rows = slice(side_at * uppers * ROWS, (side_at + 1) * uppers * ROWS)
            sums_ref[rows, :] += both[:, side_at * LANES : (side_at + 1) * LANES]

    for side_at in range(sides):
        cell = lax.broadcasted_iota(jnp.int32, (uppers, LANES), 0) * LOWER + side_at * LANES
        cell = cell + lax.broadcasted_iota(jnp.int32, (uppers, LANES), 1)
        index = [cell // (side * side), cell // side % side, cell % side]

        def summed(q):
            return sums_ref[pl.ds(side_at * uppers * ROWS + q, uppers, stride=ROWS), :]

        mass = summed(0)
        inverse = 1.0 / jnp.maximum(mass, MASS_FLOOR)
        first = [summed(1 + a) for a in range(3)]
        shift = [first[a] * inverse for a in range(3)]
        lowered = traceless(*outer(first, shift))
        centre = [(index[a].astype(f32) + 0.5) / side + shift[a] for a in range(3)]
        quad = [summed(4 + k) - lowered[k] for k in range(6)]
        write_cells(cells_ref, blocks + side_at * uppers, uppers, mass, centre, quad)

    def turn(block, start):
        values = cells_ref[block * ROWS : (block + 1) * ROWS, :]
        rows_ref[start : start + LANES, :PARTS] = jnp.transpose(in_parts(values))

    for block in range(blocks):
        turn(block, block * LANES)
    for side_at in range(sides):
        for u in range(uppers):
            start = blocks * LANES + u * LOWER + side_at * LANES
            turn(blocks + side_at * uppers + u, start)


def cell_terms(off, along, mass, sums):
    dist = off[0] * off[0] + off[1] * off[1] + off[2] * off[2] + EPS
    inv = lax.rsqrt(dist)
    inv_two = inv * inv
    inv_five = inv_two * inv_two * inv
    both = off[0] * along[0] + off[1] * along[1] + off[2] * along[2]
    radial = mass * dist + 2.5 * both * inv_two
    for a in range(3):
        sums[a] += (along[a] - radial * off[a]) * inv_five


def with_norm(values, extra, scale, last):
    squares = jnp.where(last, 0.0, values * values)
    norm = pltpu.roll(squares, 1, 0) + pltpu.roll(squares, 2, 0) + pltpu.roll(squares, 3, 0)
    return jnp.where(last, norm + extra, scale * values)


def three(values):
    high = rounded(values)
    rest = values - high
    middle = rounded(rest)
    return high, middle, rest - middle


def prepare_near(tile, sources, masses, left_ref, right_ref, pull_ref, target_ref):
    row = row_iota()
    last = row % 4 == 3
    front = row < 4
    mean = jnp.sum(tile, axis=1, keepdims=True)
    mean = jnp.broadcast_to(mean, (8, LANES))
    centre = jnp.where(last, 0.0, (mean + pltpu.roll(mean, 4, 0)) * (0.5 / LANES))
    target = tile - centre
    target_ref[...] = target
    high, middle, low = three(with_norm(target, EPS, -2.0, last))
    plain = jnp.where(last, 1.0, high)
    blocks = [plain, plain, plain, jnp.where(last, high, middle), middle, low]
    turned = [pltpu.roll(block, 4, 0) for block in blocks]
    first = [jnp.where(front, b, t) for b, t in zip(blocks, turned)]
    second = [jnp.where(front, t, b) for b, t in zip(blocks, turned)]
    for half in range(2):
        keep = front if half == 0 else jnp.logical_not(front)
        for side, parts in enumerate((first, second)):
            right_ref[half, :, side * LANES : (side + 1) * LANES] = jnp.concatenate(
                [jnp.where(keep, part, 0.0) for part in parts], axis=0
            ).astype(bf16)
    for k, (source, weights) in enumerate(zip(sources, masses)):
        at = slice(k * LANES, (k + 1) * LANES)
        place = source - centre
        high, middle, low = three(with_norm(place, 0.0, 1.0, last))
        high_one = jnp.where(last, 1.0, high)
        middle_one = jnp.where(last, 1.0, middle)
        stack = jnp.concatenate([high, middle, low, high_one, middle_one, high_one], axis=0)
        left_ref[at, :] = jnp.transpose(stack).astype(bf16)
        mass = jnp.where(last, weights, 0.0)
        mass = mass + pltpu.roll(mass, 7, 0) + pltpu.roll(mass, 6, 0) + pltpu.roll(mass, 5, 0)
        moved = mass * place
        moved_high, mass_high = rounded(moved), rounded(mass)
        pull_ref[:, at] = jnp.concatenate(
            [moved_high, moved - moved_high, mass_high, mass - mass_high], axis=0
        ).astype(bf16)


def near_distances(operand, start, width):
    left_ref, right_ref = operand[:2]
    left = left_ref[start : start + width, :]
    return [jnp.dot(left, right_ref[half], preferred_element_type=f32) for half in range(2)]


def near_pulls(operand, start, width, dist, total):
    pull = operand[2][:, start : start + width]
    weight = [lax.rsqrt((d * d * d).astype(bf16)) for d in dist]
    for half in range(2):
        part = jnp.dot(pull, weight[half], preferred_element_type=f32)
        total[half] = part if total[half] is None else total[half] + part


def near_result(target, total):
    row = row_iota()
    last = row % 4 == 3
    front = row < 4

    def fold(start):
        parts = [t[start : start + 8, :] + t[start + 8 : start + 16, :] for t in total]
        sides = []
        for side in range(2):
            at = slice(side * LANES, (side + 1) * LANES)
            mixed = jnp.where(front, parts[0][:, at], parts[1][:, at])
            sides.append(mixed + pltpu.roll(mixed, 4, 0))
        return jnp.where(front, sides[0], sides[1])

    return jnp.where(last, 0.0, fold(0) - target * fold(16))


def near_kernel(second, sub_count, bucket_count, near_count, me_ref, work_ref, list_ref, *refs):
    refs = list(refs)
    tables = [refs.pop(0) for _ in range(sub_count * CHUNKS)]
    if second:
        table_refs = [refs.pop(0) for _ in range(sub_count)]
        acc_refs = [refs.pop(0) for _ in range(sub_count)]
    both_ref = refs.pop(0)
    out_ref, tile_ref = both_ref.at[0], both_ref.at[1]
    group_ref, sem = refs[:2]
    operands = [refs[2 + 4 * k : 6 + 4 * k] for k in range(8)]
    me = me_ref[0]
    mass_ref = group_ref
    if second:
        mass_ref, acc_ref = refs[2 + 4 * 8 :]
    piece = bucket_count // CHUNKS
    copies = [
        pltpu.make_async_copy(ref, mass_ref.at[pl.ds(k * piece, piece)], sem.at[k])
        for k, ref in enumerate(tables)
    ]
    if second:
        copies += [
            pltpu.make_async_copy(
                table_refs[k],
                group_ref.at[pl.ds(k * bucket_count, bucket_count)],
                sem.at[len(tables) + k],
            )
            for k in range(sub_count)
        ]
        copies += [
            pltpu.make_async_copy(acc_refs[k], acc_ref.at[k], sem.at[len(tables) + sub_count + k])
            for k in range(sub_count)
        ]
    for copy in copies:
        copy.start()
    for copy in copies:
        copy.wait()
    if second:
        last = row_iota() % 4 == 3
        for part in range(sub_count):

            @pl.loop(0, work_ref.shape[1], unroll=4)
            def _(i):
                slot = other_slot(work_ref[part, i], bucket_count, me)
                tile = group_ref[slot]
                act = jnp.where(last, tile, 0.0)
                act = act + pltpu.roll(act, 7, 0) + pltpu.roll(act, 6, 0) + pltpu.roll(act, 5, 0)
                group_ref[slot] = tile + (DT * DT) * act * acc_ref[part, i]

    def prepare(i, slot):
        tile = group_ref[other_slot(work_ref[0, i], bucket_count, me)]
        tile_ref[i] = tile
        slots = [list_ref[i, k] for k in range(near_count)]
        prepare_near(
            tile, [group_ref[n] for n in slots], [mass_ref[n] for n in slots], *operands[slot]
        )

    count = work_ref.shape[1]
    span = 8
    width = 4 * LANES
    rows = near_count * LANES
    prepare(0, 0)

    @pl.loop(0, pl.cdiv(count, span))
    def _(block):
        steps = [(part, start) for part in range(span) for start in range(0, rows, width)]
        first = block * span
        totals = {}

        def finish(part, start, dist):
            near_pulls(operands[part], start, width, dist, totals[part])
            if start + width == rows:
                target = operands[part][3][...]
                out_ref[jnp.minimum(first + part, count - 1)] = near_result(target, totals[part])

        pending = None
        for part, start in steps:
            if start == 0:
                totals[part] = [None, None]
            if start == 0 and part + 1 < span:
                prepare(jnp.minimum(first + part + 1, count - 1), part + 1)
            dist = near_distances(operands[part], start, width)
            if pending is not None:
                finish(*pending)
            pending = (part, start, dist)
        prepare(jnp.minimum(first + span, count - 1), 0)
        finish(*pending)


def splat_operand():
    row = lax.broadcasted_iota(jnp.int32, (PARTS, LANES), 0)
    keep = jnp.logical_and(row % 8 == 6, jnp.logical_and(row >= 48, row < 72))
    return jnp.where(keep, 1.0, 0.0).astype(bf16)


def fixed_operand():
    shape = (PARTS, 12 * LANES)
    row = lax.broadcasted_iota(jnp.int32, shape, 0)
    number = lax.broadcasted_iota(jnp.int32, shape, 1) // (2 * LANES)
    keep = jnp.logical_and(row % 8 == number, jnp.logical_and(row >= 48, row < 72))
    return jnp.where(keep, -1.0, 0.0).astype(bf16)


def particle_operand(tile, places_ref):
    row = row_iota()
    parts = three(tile)
    order = (0, 1, 2, 0, 1, 0)
    for half in range(2):
        spread = [
            [jnp.broadcast_to(p[4 * half + a : 4 * half + a + 1, :], (8, LANES)) for a in range(3)]
            for p in parts
        ]
        for a in range(3):
            rows = ((0, 3, 4), (3, 1, 5), (4, 5, 2))[a]
            mixed = [
                jnp.where(
                    row == rows[0],
                    x,
                    jnp.where(row == rows[1], y, jnp.where(row == rows[2], z, 0.0)),
                )
                for x, y, z in spread
            ]
            at = (6 + 2 * a + half) * LANES
            places_ref[:48, at : at + LANES] = jnp.concatenate(
                [mixed[p] for p in order], axis=0
            ).astype(bf16)
            tail = [
                jnp.where(row == a, -1.0, jnp.where(row == 7, spread[p][a], 0.0)) for p in range(3)
            ]
            at = (2 * a + half) * LANES
            places_ref[48:, at : at + LANES] = jnp.concatenate(
                tail + [jnp.zeros((8, LANES), f32)], axis=0
            ).astype(bf16)


def cells_kernel(
    near_count,
    cell_count,
    top_count,
    list_ref,
    ess_ref,
    cells_ref,
    both_ref,
    out_ref,
    splat_ref,
    *slots,
):
    near_ref, tile_ref = both_ref.at[0], both_ref.at[1]
    rows_ref = slots[4]
    build_rows(cells_ref, *slots[4:])
    splat_ref[...] = splat_operand()
    for side in range(2):
        slots[2 * side + 1][...] = fixed_operand()
    count = both_ref.shape[1]
    total = cell_count + top_count

    def pick_rows(i, slot, start, stop):
        picked_ref = slots[2 * slot]
        for k in range(start, stop):
            index = list_ref[i, near_count + k]
            if k < cell_count:
                index = ess_ref[index]
            picked_ref[pl.ds(k, 1), :] = rows_ref[pl.ds(index, 1), :]

    def place(i, slot):
        particle_operand(tile_ref[i], slots[2 * slot + 1])

    def spread_cells(slot, start):
        picked_ref, places_ref = slots[2 * slot : 2 * slot + 2]
        left = picked_ref[start : start + CELL_CHUNK, :PARTS].astype(bf16)
        return (
            jnp.dot(left, splat_ref[...], preferred_element_type=f32),
            jnp.dot(left, places_ref[...], preferred_element_type=f32),
        )

    def finish(i, sums):
        row = row_iota()
        result = near_ref[i]
        for half in range(2):
            for a in range(3):
                value = jnp.sum(sums[half][a], axis=0, keepdims=True)
                value = jnp.broadcast_to(value, (8, LANES))
                result += jnp.where(row == 4 * half + a, value, 0.0)
        out_ref[i] = result

    pick_rows(0, 0, 0, total)
    place(0, 0)
    chunks = range(0, total, CELL_CHUNK)
    early = (len(chunks) - 1) * CELL_CHUNK // 8
    share = -(-total // early)

    @pl.loop(0, pl.cdiv(count, CELL_SPAN))
    def _(block):
        item = [jnp.minimum(CELL_SPAN * block + k, count - 1) for k in range(CELL_SPAN + 1)]
        waiting = spread_cells(0, 0)
        for step in range(CELL_SPAN):
            slot = step % 2
            sums = [[jnp.zeros((8, LANES), f32) for _ in range(3)] for _ in range(2)]
            done = 0
            place(item[step + 1], 1 - slot)
            for start in chunks:
                splats, offs = waiting
                if start + CELL_CHUNK < total:
                    waiting = spread_cells(slot, start + CELL_CHUNK)
                elif step + 1 < CELL_SPAN:
                    waiting = spread_cells(1 - slot, 0)
                for group in range(CELL_CHUNK // 8):
                    rows = slice(8 * group, 8 * group + 8)
                    for half in range(2):
                        off, along = [
                            [
                                offs[rows, at * LANES : (at + 1) * LANES]
                                for at in range(first + half, first + 6, 2)
                            ]
                            for first in (0, 6)
                        ]
                        cell_terms(off, along, splats[rows], sums[half])
                    if done < total:
                        pick_rows(item[step + 1], 1 - slot, done, min(done + share, total))
                        done += share
            finish(item[step], sums)


def body(
    positions,
    velocities,
    masses,
    accel_prev,
    active,
    bucket_top,
    near_list,
    cell_list,
    top_list,
    essential,
    work,
):
    bucket_count = bucket_top.shape[0]
    sub_count = lax.axis_size("sub")
    dom_count = lax.axis_size("dom")
    me = lax.axis_index("sub").astype(jnp.int32)
    group_buckets = sub_count * bucket_count
    device_count = sub_count * dom_count
    near_count, cell_count, top_count = near_list.shape[1], cell_list.shape[1], top_list.shape[1]
    work_count = work.shape[0]
    vmem = pl.BlockSpec(memory_space=pltpu.VMEM)
    smem = pl.BlockSpec(memory_space=pltpu.SMEM)
    anywhere = pl.BlockSpec(memory_space=pl.ANY)
    work_shape = jax.ShapeDtypeStruct((work_count, 8, LANES), f32)
    sent_shape = jax.ShapeDtypeStruct((device_count * bucket_count // LANES * SENT, LANES), f32)

    activity = active.astype(f32)
    half_speed = velocities + 0.5 * DT * activity * accel_prev
    places = positions + DT * half_speed
    tiles = to_tiles(places, masses)
    places, half_speed, activity, _ = lax.optimization_barrier(
        (places, half_speed, activity, tiles)
    )
    ahead = to_tiles(places + DT * half_speed, activity)
    speeds = to_tiles(half_speed, activity)

    tops_row = bucket_top.astype(f32)[None]

    own = pl.pallas_call(
        first_moments_kernel,
        out_shape=sent_shape,
        in_specs=[vmem] * 2,
        out_specs=vmem,
        compiler_params=pltpu.CompilerParams(vmem_limit_bytes=20 << 20),
        name="first_moments",
    )(tiles.reshape(-1, LANES), tops_row)

    def exchange(rows):
        wide = rows.reshape(device_count, -1)
        got = lax.all_to_all(wide, ("dom", "sub"), split_axis=0, concat_axis=0, tiled=True)
        return got.reshape(-1, LANES)

    cells = exchange(own)
    near_list, cell_list, top_list, essential, work, _ = lax.optimization_barrier(
        (near_list, cell_list, top_list, essential, work, (own, ahead, speeds))
    )

    def as_rows(values):
        return jnp.pad(values, (0, -values.shape[0] % LANES)).reshape(-1, LANES)

    lists = jnp.concatenate([near_list, cell_list, top_list], axis=1)
    lists = jnp.pad(lists, ((0, 0), (0, -lists.shape[1] % LANES)))
    width = lists.shape[1]
    wanted = essential.reshape(dom_count, -1) + (
        jnp.arange(dom_count, dtype=jnp.int32) * group_buckets
    )[:, None]
    ess_size = wanted.size
    list_rows = bucket_count * width // LANES
    ess_rows = -(-ess_size // LANES)
    sent = jnp.concatenate(
        [lists.reshape(-1, LANES), as_rows(wanted.reshape(-1)), as_rows(work)], axis=0
    )
    sent_rows = sent.shape[0]
    sent = jnp.pad(sent, ((0, -sent_rows % 8), (0, 0)))
    all_rows = jnp.stack(sub_gather(sent, sub_count))
    ess_all = all_rows[:, list_rows : list_rows + ess_rows].reshape(sub_count, -1)
    ess_all = ess_all[:, :ess_size].reshape(-1)
    work_all = all_rows[:, list_rows + ess_rows : sent_rows].reshape(sub_count, -1)
    work_all = work_all[:, :work_count]
    mine = other_slot(work, bucket_count, me)
    if width == LANES:
        index = mine // bucket_count * sent.shape[0] + mine % bucket_count
        work_lists = jnp.take(all_rows.reshape(-1, LANES), index, axis=0)
    else:
        list_table = all_rows[:, :list_rows].reshape(group_buckets, width)
        work_lists = jnp.take(list_table, mine, axis=0)
    column = jnp.arange(width)[None]
    work_lists = jnp.where(
        column < near_count,
        other_slot(work_lists, bucket_count, me),
        jnp.where(
            column < near_count + cell_count,
            other_slot(work_lists, ess_size, me),
            work_lists + device_count * bucket_count,
        ),
    )
    piece = bucket_count // CHUNKS
    pieces = [sub_gather(tiles[c * piece : (c + 1) * piece], sub_count, work_lists) for c in range(CHUNKS)]
    table = [pieces[c][k] for k in range(sub_count) for c in range(CHUNKS)]
    ahead_sent, _ = lax.optimization_barrier((ahead, table))
    table_ahead = sub_gather(ahead_sent, sub_count)

    me_one = me[None]

    def near_call(second, extra_tables):
        operand = [
            pltpu.VMEM((near_count * LANES, 48), bf16),
            pltpu.VMEM((2, 48, 2 * LANES), bf16),
            pltpu.VMEM((32, near_count * LANES), bf16),
            pltpu.VMEM((8, LANES), f32),
        ]
        scratch = [
            pltpu.VMEM((group_buckets, 8, LANES), f32),
            pltpu.SemaphoreType.DMA(((2 + CHUNKS) * sub_count,)),
        ] + operand * 8
        specs = [smem] * 3 + [anywhere] * (sub_count * CHUNKS)
        if second:
            specs += [anywhere] * (2 * sub_count)
            scratch += [
                pltpu.VMEM((group_buckets, 8, LANES), f32),
                pltpu.VMEM((sub_count, work_count, 8, LANES), f32),
            ]
        return pl.pallas_call(
            functools.partial(near_kernel, second, sub_count, bucket_count, near_count),
            out_shape=jax.ShapeDtypeStruct((2, *work_shape.shape), f32),
            in_specs=specs,
            out_specs=vmem,
            scratch_shapes=scratch,
            compiler_params=pltpu.CompilerParams(vmem_limit_bytes=20 << 20),
            name="near_second" if second else "near_first",
        )(me_one, work_all, work_lists, *table, *extra_tables)

    def cells_call(cells, both):
        buckets = cells.shape[0] // SENT * LANES
        scratch = [pltpu.VMEM((PARTS, LANES), bf16)] + [
            pltpu.VMEM((cell_count + top_count, LANES), f32),
            pltpu.VMEM((PARTS, 12 * LANES), bf16),
        ] * 2
        scratch += [
            pltpu.VMEM((buckets + TOP, LANES), f32),
            pltpu.VMEM((ROWS * buckets // LANES, LANES), f32),
            pltpu.VMEM((TOP // LANES * ROWS, LANES), f32),
            pltpu.VMEM(((buckets + TOP) // LANES * ROWS, LANES), f32),
        ]
        return pl.pallas_call(
            functools.partial(cells_kernel, near_count, cell_count, top_count),
            out_shape=work_shape,
            in_specs=[smem] * 2 + [vmem] * 2,
            out_specs=vmem,
            scratch_shapes=scratch,
            compiler_params=pltpu.CompilerParams(vmem_limit_bytes=24 << 20),
            name="cell_force",
        )(work_lists, ess_all, cells, both)

    near = near_call(False, [])
    acc_one = sub_gather(cells_call(cells, near), sub_count)
    flat_shape = jax.ShapeDtypeStruct((bucket_count * 8, LANES), f32)
    own_shape = jax.ShapeDtypeStruct(((bucket_count + 1) * 8, LANES), f32)

    def flat(values):
        return values.reshape(-1, LANES)

    own, places_two, base = pl.pallas_call(
        functools.partial(second_moments_kernel, sub_count),
        out_shape=(sent_shape, flat_shape, flat_shape),
        in_specs=[smem] * 2 + [vmem] * (4 + sub_count),
        out_specs=(vmem,) * 3,
        scratch_shapes=[pltpu.VMEM(own_shape.shape, f32)],
        compiler_params=pltpu.CompilerParams(vmem_limit_bytes=20 << 20),
        name="second_moments",
    )(me_one, work_all, flat(ahead), flat(tiles), flat(speeds), tops_row, *acc_one)
    cells = exchange(own)
    near = near_call(True, [*table_ahead, *acc_one])
    acc_two = sub_gather(cells_call(cells, near), sub_count)
    speed_two = pl.pallas_call(
        functools.partial(final_kernel, sub_count),
        out_shape=flat_shape,
        in_specs=[smem] * 2 + [vmem] * (1 + sub_count),
        out_specs=vmem,
        scratch_shapes=[pltpu.VMEM(own_shape.shape, f32)],
        compiler_params=pltpu.CompilerParams(vmem_limit_bytes=20 << 20),
        name="final_speeds",
    )(me_one, work_all, base, *acc_two)
    return (
        from_tiles(speed_two.reshape(-1, 8, LANES)),
        from_tiles(places_two.reshape(-1, 8, LANES)),
    )


def solution(mesh):
    both = ("dom", "sub")
    in_specs = (
        P(None, both),
        P(None, both),
        P(both),
        P(None, both),
        P(both),
        P(both),
        P(both, None),
        P(both, None),
        P(both, None),
        P("dom", "sub", None, None),
        P(both),
    )
    out_specs = (P(None, both), P(None, both))

    return jax.shard_map(body, mesh=mesh, in_specs=in_specs, out_specs=out_specs, check_vma=False)
```
